32 devices in a mesh: groups: 2 (over y), energy: 4 (over z), tile: 2 (over x), mode: 2 (over core).
Axes of the slice: x: 2, y: 2, z: 4, core: 2. Of those that a mesh axis runs over, the one named last changes fastest.
Arguments:
- object_field: float32 [2, 16, 256, 192], P(None, ('groups', 'energy', 'mode'), 'tile'), parts along dimension 1, may hold values from -6 to 6
- probe_field: float32 [2, 3, 16, 128, 128], P(None, None, ('groups', 'energy', 'mode')), parts along dimension 2, may hold values from -6 to 6
- modulus: bfloat16 [16, 16, 128, 128], P(('groups', 'energy', 'mode'), 'tile'), parts along dimension 0, may hold values from 0 to 2
- offsets: int32 [32, 2], P(('groups', 'tile')), parts along dimension 0, may hold values from 0 to 31
- spectra_basis: float32 [8, 8], replicated, may hold values from -2 to 2
- analysis: float32 [8, 8], replicated, may hold values from -2 to 2
- threshold: float32 [8], replicated, may hold values from 0.05 to 0.5
Outputs:
- object_out: float32 [2, 16, 256, 192], P(None, ('groups', 'energy', 'mode'), 'tile'), parts along dimension 1
- probe_out: float32 [2, 3, 16, 128, 128], P(None, None, ('groups', 'energy', 'mode')), parts along dimension 2
The draws below stay inside these ranges and needn't reach their ends.
There are 2 independent parts, one for each index of `groups`. The reference program is written for one: setup_inputs(seed, part) draws one part's arguments, and reference() takes and returns one part's arrays. A program takes and returns all parts, laid end to end along the dimension named above; an argument that names none is the same for every part. Nothing has to cross between parts.
All inputs are finite; a program needn't handle non-finite values.
Results may differ from the reference program's by a relative error of at most 0.0033.
Values may be sent and summed in bfloat16 or wider, within the bound.
No kernel may reach another device: no remote copies, remote signals or barrier semaphores. Data moves between devices by JAX's collectives and lax.ppermute only.
A program may use at most 128 MiB of HBM per device.

```python
import math
import jax
import jax.numpy as jnp
from jax import lax

PSIZE = 128
MODES = 3
COMPS = 8
ITERS = 1
PCOLS = 2
STEP = 32
TILE_ROWS = 128
WIDTH_COLS = 192
ROWS_ALL = 256
POS_DEV = 8
POS = 16
ENERGIES = 8


def touch_ends(result, key, smallest, high):
    place = [jax.random.randint(jax.random.fold_in(key, axis), (), 0, length) for axis, length in enumerate(result.shape)]
    longest = result.shape.index(max(result.shape))
    neighbour = place[:longest] + [(place[longest] + 1) % result.shape[longest]] + place[longest + 1:]
    return result.at[tuple(place)].set(smallest).at[tuple(neighbour)].set(high)


def block_scale(rng, dims, split, smallest, largest):
    def one(dim, blocks):
        heights = jax.random.uniform(jax.random.fold_in(jax.random.fold_in(rng, 6), dim), (blocks,), jnp.float32, smallest / len(split), largest / len(split))
        return jnp.repeat(jnp.exp(heights), dims[dim] // blocks).reshape((-1,) + (1,) * (len(dims) - dim - 1))

    gain = one(*split[0])
    for cut in split[1:]:
        gain = gain * one(*cut)
    return gain


def scatter_about(own_key, dims, deviation, limit, shards=(), held_as=jnp.bfloat16):
    values = jax.random.normal(own_key, dims, jnp.float32) * deviation
    if len(shards) > 0:
        values = block_scale(own_key, dims, shards, -0.22, 0.18) * values
    return jnp.clip(values, min=-limit, max=limit).astype(held_as)


def setup_inputs(seed: int = 0, part: int = 0) -> dict:
    splits = jax.random.split(jax.random.key(seed), 8)
    part_keys = jax.random.split(jax.random.fold_in(splits[7], part), 8)
    object_field = scatter_about(part_keys[0], (2, ENERGIES, ROWS_ALL, WIDTH_COLS), 1.0, 6.0, ((1, 8), (2, 2)), jnp.float32)
    probe_field = scatter_about(part_keys[1], (2, MODES, ENERGIES, PSIZE, PSIZE), 0.6, 6.0, ((2, 8),), jnp.float32)
    modulus = jnp.clip(2.0 * jax.random.uniform(part_keys[2], (ENERGIES, POS, PSIZE, PSIZE), jnp.float32) ** block_scale(part_keys[2], (ENERGIES, POS, PSIZE, PSIZE), ((0, 8), (1, 2)), -0.2, 0.2), 0.0, 2.0).astype(jnp.bfloat16)
    offsets = touch_ends(jax.random.randint(part_keys[3], (POS, 2), 0, STEP), jax.random.fold_in(part_keys[3], 1), 0, STEP - 1).astype(jnp.int32)
    spectra_basis = scatter_about(splits[4], (ENERGIES, COMPS), COMPS ** -0.5, 2.0, (), jnp.float32)
    analysis = scatter_about(splits[5], (COMPS, ENERGIES), ENERGIES ** -0.5, 2.0, (), jnp.float32)
    threshold = jnp.clip(jnp.exp(jax.random.uniform(splits[6], (COMPS,), jnp.float32, math.log(0.05), math.log(0.5))), 0.05, 0.5)
    return {"object_field": object_field, "probe_field": probe_field, "modulus": modulus, "offsets": offsets, "spectra_basis": spectra_basis, "analysis": analysis, "threshold": threshold}


per_block = 8

def dft_tables(extent):
    counter = jnp.arange(extent, dtype=jnp.int32)
    products_mod = counter[:, None] * counter[None, :] % extent
    phases = -2.0 * math.pi / extent * products_mod.astype(jnp.float32)
    normalizer = 1.0 / math.sqrt(extent)
    cosine = jnp.cos(phases) * normalizer
    sine_table = jnp.sin(phases) * normalizer
    forward = jnp.concatenate([jnp.concatenate([cosine, -sine_table], axis=1), jnp.concatenate([sine_table, cosine], axis=1)], axis=0).astype(jnp.bfloat16)
    backward = jnp.concatenate([jnp.concatenate([cosine, sine_table], axis=1), jnp.concatenate([-sine_table, cosine], axis=1)], axis=0).astype(jnp.bfloat16)
    return (forward, backward)

def product(form, left_op, right_op):
    return jnp.einsum(form, left_op.astype(jnp.float32), right_op.astype(jnp.float32))

def wave_block(extended, probe_now, block_moduli, row_starts, col_starts, tables, multiply):
    extent = probe_now.shape[-1]
    members = block_moduli.shape[0]
    modes_here = probe_now.shape[1]
    anchor = jnp.zeros((), jnp.int32)

    def cut_patch(row_start, col_start):
        return lax.dynamic_slice(extended, (anchor, row_start, col_start), (2, extent, extent))
    patches = jax.vmap(cut_patch)(row_starts, col_starts)
    object_real = patches[:, 0:1]
    object_imag = patches[:, 1:2]
    probe_real = probe_now[0][None]
    probe_imag = probe_now[1][None]
    wave_real = probe_real * object_real - probe_imag * object_imag
    wave_imag = probe_real * object_imag + probe_imag * object_real
    stacked = jnp.concatenate([wave_real, wave_imag], axis=2)
    forward, backward = tables
    batch = stacked.reshape(members * modes_here, 2 * extent, extent).astype(jnp.bfloat16)
    halfway = multiply('ij,bjk->bik', forward, batch)
    columns = jnp.concatenate([halfway[:, :extent], halfway[:, extent:]], axis=2).astype(jnp.bfloat16)
    spectrum = multiply('bik,kl->bil', columns, backward).reshape(members, modes_here, extent, 2 * extent)
    squares = lax.optimization_barrier(jnp.sum(spectrum * spectrum, axis=1))
    magnitude_sq = squares[:, :, :extent] + squares[:, :, extent:]
    factor = block_moduli.astype(spectrum.dtype) / jnp.sqrt(magnitude_sq + 0.01)
    scaled = (spectrum * jnp.concatenate([factor, factor], axis=2)[:, None]).astype(jnp.bfloat16)
    scaled = scaled.reshape(members * modes_here, extent, 2 * extent)
    returned = multiply('bik,kl->bil', scaled, forward)
    restacked = jnp.concatenate([returned[:, :, :extent], returned[:, :, extent:]], axis=1).astype(jnp.bfloat16)
    new_wave = multiply('ij,bjk->bik', backward, restacked).reshape(members, modes_here, 2 * extent, extent)
    change = new_wave - stacked
    change_real = change[:, :, :extent]
    change_imag = change[:, :, extent:]
    numerator = jnp.stack([lax.optimization_barrier(jnp.sum(probe_real * change_real + probe_imag * change_imag, axis=1)), lax.optimization_barrier(jnp.sum(probe_real * change_imag - probe_imag * change_real, axis=1))], axis=1)
    probe_num = jnp.stack([lax.optimization_barrier(jnp.sum(object_real * change_real + object_imag * change_imag, axis=0)), lax.optimization_barrier(jnp.sum(object_real * change_imag - object_imag * change_real, axis=0))], axis=0)
    probe_den = lax.optimization_barrier(jnp.sum(object_real * object_real + object_imag * object_imag, axis=(0, 1)))
    return (numerator, probe_num, probe_den)

def accumulate(extended, probe_now, probe_power, moduli, row_starts, col_starts, tables, multiply):
    extent = probe_now.shape[-1]
    blocks = moduli.shape[0] // per_block
    anchor = jnp.zeros((), jnp.int32)

    def one_block(running, operands):
        sum_wave, sum_weight, probe_num, probe_den = running
        block_moduli, block_rows, block_cols = operands
        numerator, block_num, block_den = wave_block(extended, probe_now, block_moduli, block_rows, block_cols, tables, multiply)
        for member in range(per_block):
            corner = (anchor, block_rows[member], block_cols[member])
            sum_wave = lax.dynamic_update_slice(sum_wave, lax.dynamic_slice(sum_wave, corner, (2, extent, extent)) + numerator[member], corner)
            flat_corner = (block_rows[member], block_cols[member])
            sum_weight = lax.dynamic_update_slice(sum_weight, lax.dynamic_slice(sum_weight, flat_corner, (extent, extent)) + probe_power, flat_corner)
        return ((sum_wave, sum_weight, probe_num + block_num, probe_den + block_den), None)
    start_state = (jnp.zeros_like(extended), jnp.zeros(extended.shape[1:], extended.dtype), jnp.zeros_like(probe_now), jnp.zeros((extent, extent), probe_now.dtype))
    operands = (moduli.reshape(blocks, per_block, extent, extent), row_starts.reshape(blocks, per_block), col_starts.reshape(blocks, per_block))
    final_state, unused = lax.scan(one_block, start_state, operands)
    return final_state

def spectral(spectra, spectra_basis, analysis, threshold):
    coefficient = jnp.einsum('ke,xep->xkp', analysis, spectra, precision=lax.Precision.HIGHEST)
    shrunk = jnp.sign(coefficient) * jnp.maximum(jnp.abs(coefficient) - threshold[None, :, None], 0.0)
    projected = jnp.einsum('ek,xkp->xep', spectra_basis, shrunk, precision=lax.Precision.HIGHEST)
    return 0.5 * spectra + 0.5 * projected

def reference(object_field, probe_field, modulus, offsets, spectra_basis, analysis, threshold):
    extent = PSIZE
    tables = dft_tables(extent)
    counter = jnp.arange(POS, dtype=jnp.int32)
    within = counter % POS_DEV
    owner_tile = counter // POS_DEV
    row_starts = (owner_tile * TILE_ROWS + STEP * (within // PCOLS) + offsets[:, 0]).astype(jnp.int32)
    col_starts = (STEP * (within % PCOLS) + offsets[:, 1]).astype(jnp.int32)
    object_now = jnp.transpose(object_field, (1, 0, 2, 3))
    probe_now = jnp.transpose(probe_field, (2, 0, 1, 3, 4))
    for sweep in range(ITERS):

        def one_energy(operands):
            object_e, probe_e, moduli_e = operands
            rounded = lax.optimization_barrier(object_e.astype(jnp.bfloat16)).astype(object_e.dtype)
            extended = jnp.pad(rounded, ((0, 0), (0, extent), (0, 0)))
            probe_power = lax.optimization_barrier(jnp.sum(probe_e * probe_e, axis=(0, 1)))
            sum_wave, sum_weight, probe_num, probe_den = accumulate(extended, probe_e, probe_power, moduli_e, row_starts, col_starts, tables, product)
            object_new = object_e + sum_wave[:, :ROWS_ALL] / (sum_weight[:ROWS_ALL] + 0.1 * jnp.max(probe_power) + 1e-06)
            probe_new = probe_e + probe_num / (probe_den + 0.1 * jnp.max(probe_den) + 1e-06)
            return (object_new, probe_new)
        object_now, probe_now = lax.map(one_energy, (object_now, probe_now, modulus))
        spectra = jnp.transpose(object_now, (1, 0, 2, 3)).reshape(2, ENERGIES, ROWS_ALL * WIDTH_COLS)
        spectra = spectral(spectra, spectra_basis, analysis, threshold)
        object_now = jnp.transpose(spectra.reshape(2, ENERGIES, ROWS_ALL, WIDTH_COLS), (1, 0, 2, 3))
    return (jnp.transpose(object_now, (1, 0, 2, 3)), jnp.transpose(probe_now, (1, 2, 0, 3, 4)))
```

```python
import functools
import math

import jax
import jax.numpy as jnp
import ml_dtypes
import numpy as np
from jax import lax
from jax.experimental import pallas as pl
from jax.experimental.pallas import tpu as pltpu
from jax.sharding import PartitionSpec as P

PCOLS = 2
STEP = 32
LANES = 128
PAD_ROWS = 16

VMEM = pl.BlockSpec(memory_space=pltpu.VMEM)
SMEM = pl.BlockSpec(memory_space=pltpu.SMEM)


def swap_pairs(size, distance):
    return [(i, i ^ distance) for i in range(size)]


def power_of_two(size):
    return size & (size - 1) == 0


def dft_tables(extent):
    counter = np.arange(extent)
    phases = -2.0 * math.pi / extent * (counter[:, None] * counter[None, :] % extent)
    cosine = np.cos(phases) / math.sqrt(extent)
    sine = np.sin(phases) / math.sqrt(extent)
    forward = np.block([[cosine, -sine], [sine, cosine]])
    backward = np.block([[cosine, sine], [-sine, cosine]])
    return (
        jnp.asarray(forward.astype(np.float32).astype(ml_dtypes.bfloat16)),
        jnp.asarray(backward.astype(np.float32).astype(ml_dtypes.bfloat16)),
    )


def corner(offsets_ref, q):
    row = STEP * (q // PCOLS) + offsets_ref[q, 0]
    col = STEP * (q % PCOLS) + offsets_ref[q, 1]
    return row, col


def spread(block, col):
    lane = lax.broadcasted_iota(jnp.int32, block.shape, 1)
    turned = pltpu.roll(block, col, 1)
    left = jnp.where(lane >= col, turned, 0.0)
    right = jnp.where(lane < col, turned, 0.0)
    return left, right


def round_kernel(offsets_ref, object_ref, message_ref):
    rows, cols = object_ref.shape[2:]
    positions = offsets_ref.shape[0]
    for part in range(2):
        message_ref[part, :rows] = object_ref[part, 0].astype(jnp.bfloat16)
    lane = lax.broadcasted_iota(jnp.int32, (PAD_ROWS, cols), 1)
    line = jnp.zeros((PAD_ROWS, cols), jnp.float32)
    for q in range(positions):
        for k in range(2):
            value = offsets_ref[q, k].astype(jnp.float32)
            line = jnp.where(lane == 2 * q + k, value, line)
    for part in range(2):
        message_ref[part, rows:] = line.astype(jnp.bfloat16)


def wave_kernel(
    offsets_ref,
    own_ref,
    below_ref,
    probe_ref,
    moduli_ref,
    forward_ref,
    backward_ref,
    upper_ref,
    lower_ref,
    share_ref,
    extended,
    total,
    window,
    stacked,
    batch,
    columns,
    probe_num,
    probe_den,
    *,
    tiles,
    group,
):
    extent = probe_ref.shape[-1]
    modes = probe_ref.shape[1]
    rows = own_ref.shape[1] - PAD_ROWS
    cols = own_ref.shape[2]
    positions = offsets_ref.shape[0]
    has_below = lax.axis_index("tile") < tiles - 1
    for part in range(2):
        own = own_ref[part, :rows].astype(jnp.float32)
        below = jnp.where(has_below, below_ref[part, :rows].astype(jnp.float32), 0.0)
        for side, first in enumerate(range(0, cols, LANES)):
            last = min(first + LANES, cols)
            extended[part, side, :rows, : last - first] = own[:, first:last]
            extended[part, side, rows:, : last - first] = below[:, first:last]
    total[...] = jnp.zeros_like(total)
    probe_num[...] = jnp.zeros_like(probe_num)
    probe_den[...] = jnp.zeros_like(probe_den)
    lane = lax.broadcasted_iota(jnp.int32, (extent, extent), 1)

    def step(block, carry):
        for member in range(group):
            q = block * group + member
            row, col = corner(offsets_ref, q)
            here = pl.ds(row, extent)
            for part in range(2):
                left = pltpu.roll(extended[part, 0, here], extent - col, 1)
                right = pltpu.roll(extended[part, 1, here], extent - col, 1)
                window[member, part] = jnp.where(lane < extent - col, left, right)
            object_real = window[member, 0]
            object_imag = window[member, 1]
            probe_den[...] += object_real * object_real + object_imag * object_imag
            for m in range(modes):
                w = member * modes + m
                probe_real = probe_ref[0, m, 0]
                probe_imag = probe_ref[1, m, 0]
                wave_real = probe_real * object_real - probe_imag * object_imag
                wave_imag = probe_real * object_imag + probe_imag * object_real
                stacked[w, :extent] = wave_real
                stacked[w, extent:] = wave_imag
                place = slice(w * extent, (w + 1) * extent)
                batch[:extent, place] = wave_real.astype(jnp.bfloat16)
                batch[extent:, place] = wave_imag.astype(jnp.bfloat16)
        halfway = jnp.dot(forward_ref[...], batch[...], preferred_element_type=jnp.float32)
        for w in range(group * modes):
            place = slice(w * extent, (w + 1) * extent)
            columns[place, :extent] = halfway[:extent, place].astype(jnp.bfloat16)
            columns[place, extent:] = halfway[extent:, place].astype(jnp.bfloat16)
        spectrum = jnp.dot(columns[...], backward_ref[...], preferred_element_type=jnp.float32)
        for member in range(group):
            q = block * group + member
            magnitude = jnp.full((extent, extent), 0.01, jnp.float32)
            for m in range(modes):
                w = member * modes + m
                place = slice(w * extent, (w + 1) * extent)
                real = spectrum[place, :extent]
                imag = spectrum[place, extent:]
                magnitude += real * real + imag * imag
            factor = moduli_ref[0, q].astype(jnp.float32) * lax.rsqrt(magnitude)
            for m in range(modes):
                w = member * modes + m
                place = slice(w * extent, (w + 1) * extent)
                real = spectrum[place, :extent]
                imag = spectrum[place, extent:]
                columns[place, :extent] = (real * factor).astype(jnp.bfloat16)
                columns[place, extent:] = (imag * factor).astype(jnp.bfloat16)
        returned = jnp.dot(columns[...], forward_ref[...], preferred_element_type=jnp.float32)
        for w in range(group * modes):
            place = slice(w * extent, (w + 1) * extent)
            batch[:extent, place] = returned[place, :extent].astype(jnp.bfloat16)
            batch[extent:, place] = returned[place, extent:].astype(jnp.bfloat16)
        new_wave = jnp.dot(backward_ref[...], batch[...], preferred_element_type=jnp.float32)
        for member in range(group):
            q = block * group + member
            row, col = corner(offsets_ref, q)
            here = pl.ds(row, extent)
            object_real = window[member, 0]
            object_imag = window[member, 1]
            sum_real = jnp.zeros((extent, extent), jnp.float32)
            sum_imag = jnp.zeros((extent, extent), jnp.float32)
            for m in range(modes):
                w = member * modes + m
                place = slice(w * extent, (w + 1) * extent)
                change_real = new_wave[:extent, place] - stacked[w, :extent]
                change_imag = new_wave[extent:, place] - stacked[w, extent:]
                probe_real = probe_ref[0, m, 0]
                probe_imag = probe_ref[1, m, 0]
                sum_real += probe_real * change_real + probe_imag * change_imag
                sum_imag += probe_real * change_imag - probe_imag * change_real
                probe_num[0, m] += object_real * change_real + object_imag * change_imag
                probe_num[1, m] += object_real * change_imag - object_imag * change_real
            for part, value in enumerate((sum_real, sum_imag)):
                for side, moved in enumerate(spread(value, col)):
                    total[part, side, here] += moved
        return carry

    lax.fori_loop(0, positions // group, step, 0)
    for part in range(2):
        for side, first in enumerate(range(0, cols, LANES)):
            last = min(first + LANES, cols)
            upper_ref[part, :, first:last] = total[part, side, :rows, : last - first]
            lower_ref[part, :, first:last] = total[part, side, rows:, : last - first].astype(
                jnp.bfloat16
            )
        for m in range(modes):
            share_ref[part * modes + m] = probe_num[part, m].astype(jnp.bfloat16)
    share_ref[2 * modes] = probe_den[...].astype(jnp.bfloat16)


def weight_kernel(offsets_ref, above_ref, probe_ref, inverse_ref, own, other):
    extent = probe_ref.shape[-1]
    modes = probe_ref.shape[1]
    rows, cols = inverse_ref.shape
    positions = offsets_ref.shape[0]
    power = jnp.zeros((extent, extent), jnp.float32)
    for part in range(2):
        for m in range(modes):
            value = probe_ref[part, m, 0]
            power += value * value
    largest = jnp.max(power)
    own[...] = jnp.zeros_like(own)
    other[...] = jnp.zeros_like(other)
    for table, place in ((offsets_ref, own), (above_ref, other)):
        for q in range(positions):
            row, col = corner(table, q)
            here = pl.ds(row, extent)
            for side, moved in enumerate(spread(power, col)):
                place[side, here] += moved
    has_above = lax.axis_index("tile") > 0
    for side, first in enumerate(range(0, cols, LANES)):
        last = min(first + LANES, cols)
        extra = jnp.where(has_above, other[side, rows:], 0.0)
        inverse = 1.0 / (own[side, :rows] + extra + 0.1 * largest + 1e-06)
        inverse_ref[:, first:last] = inverse[:, : last - first]


def object_kernel(object_ref, upper_ref, received_ref, inverse_ref, new_ref, sent_ref):
    has_above = lax.axis_index("tile") > 0
    for part in range(2):
        received = received_ref[part].astype(jnp.float32)
        wave = upper_ref[part] + jnp.where(has_above, received, 0.0)
        value = object_ref[part, 0] + wave * inverse_ref[...]
        new_ref[part] = value
        sent_ref[part] = value.astype(jnp.bfloat16)


def spectral_kernel(basis_ref, analysis_ref, threshold_ref, own_ref, *refs, sources, sizes):
    others, out_ref = refs[:-1], refs[-1]
    parts, rows, cols = own_ref.shape
    components = threshold_ref.shape[0]
    zs, ms = sizes
    z = lax.axis_index("energy")
    m = lax.axis_index("mode")
    mine = z * ms + m
    labels = [(z ^ dz) * ms + (m ^ dm) for dz, dm in sources]
    chunk = 16
    per_part = rows // chunk

    def step(index, carry):
        part = index // per_part
        here = pl.ds(pl.multiple_of((index % per_part) * chunk, chunk), chunk)
        own = own_ref[part, here]
        values = [own] + [ref[part, here].astype(jnp.float32) for ref in others]
        projected = 0.5 * own
        for k in range(components):
            c = analysis_ref[k, mine] * values[0]
            for label, value in zip(labels, values[1:]):
                c += analysis_ref[k, label] * value
            t = threshold_ref[k]
            c = c - jnp.minimum(jnp.maximum(c, -t), t)
            projected += (0.5 * basis_ref[mine, k]) * c
        out_ref[part, 0, here] = projected
        return carry

    lax.fori_loop(0, parts * per_part, step, 0)


def probe_kernel(probe_ref, own_ref, received_ref, out_ref):
    modes = probe_ref.shape[1]
    density = own_ref[2 * modes].astype(jnp.float32) + received_ref[2 * modes].astype(jnp.float32)
    inverse = 1.0 / (density + 0.1 * jnp.max(density) + 1e-06)
    for part in range(2):
        for m in range(modes):
            k = part * modes + m
            numerator = own_ref[k].astype(jnp.float32) + received_ref[k].astype(jnp.float32)
            out_ref[part, m, 0] = probe_ref[part, m, 0] + numerator * inverse


def call(kernel, inputs, scalars, outputs, scratch=(), cost=0, name=None):
    return pl.pallas_call(
        kernel,
        out_shape=outputs,
        in_specs=[SMEM] * scalars + [VMEM] * (len(inputs) - scalars),
        out_specs=jax.tree.map(lambda _: VMEM, outputs),
        scratch_shapes=list(scratch),
        name=name,
    )(*inputs)


def body(object_field, probe_field, modulus, offsets, spectra_basis, analysis, threshold):
    extent = probe_field.shape[-1]
    modes = probe_field.shape[1]
    rows, cols = object_field.shape[2:]
    positions = offsets.shape[0]
    tiles = lax.axis_size("tile")
    zs = lax.axis_size("energy")
    ms = lax.axis_size("mode")
    forward, backward = dft_tables(extent)
    shape = jax.ShapeDtypeStruct
    f32, bf16 = jnp.float32, jnp.bfloat16
    sides = pl.cdiv(cols, LANES)

    message = call(
        round_kernel, (offsets, object_field), 1, shape((2, rows + PAD_ROWS, cols), bf16), name="round"
    )
    if tiles == 2:
        below = above = lax.ppermute(message, "tile", swap_pairs(2, 1))
    else:
        below = lax.ppermute(message, "tile", [(i + 1, i) for i in range(tiles - 1)])
        above = lax.ppermute(message, "tile", [(i, i + 1) for i in range(tiles - 1)])
    above_offsets = above[0, rows, : 2 * positions].astype(jnp.int32).reshape(positions, 2)

    group = 2
    waves = group * modes
    upper, lower, share = call(
        functools.partial(wave_kernel, tiles=tiles, group=group),
        (offsets, message, below, probe_field, modulus, forward, backward),
        1,
        (
            shape((2, rows, cols), f32),
            shape((2, rows, cols), bf16),
            shape((2 * modes + 1, extent, extent), bf16),
        ),
        (
            pltpu.VMEM((2, sides, rows + extent, LANES), f32),
            pltpu.VMEM((2, sides, rows + extent, LANES), f32),
            pltpu.VMEM((group, 2, extent, extent), f32),
            pltpu.VMEM((waves, 2 * extent, extent), f32),
            pltpu.VMEM((2 * extent, waves * extent), bf16),
            pltpu.VMEM((waves * extent, 2 * extent), bf16),
            pltpu.VMEM((2, modes, extent, extent), f32),
            pltpu.VMEM((extent, extent), f32),
        ),
        name="wave",
    )
    if tiles == 2:
        received = lax.ppermute(lower, "tile", swap_pairs(2, 1))
    else:
        received = lax.ppermute(lower, "tile", [(i, i + 1) for i in range(tiles - 1)])
    inverse = call(
        weight_kernel,
        (offsets, above_offsets, probe_field),
        2,
        shape((rows, cols), f32),
        (
            pltpu.VMEM((sides, rows + extent, LANES), f32),
            pltpu.VMEM((sides, rows + extent, LANES), f32),
        ),
        name="weight",
    )
    object_new, sent = call(
        object_kernel,
        (object_field, upper, received, inverse),
        0,
        (shape((2, rows, cols), f32), shape((2, rows, cols), bf16)),
        name="object",
    )
    sources = []
    arrived = []
    for dz in range(zs):
        piece = sent if dz == 0 else lax.ppermute(sent, "energy", swap_pairs(zs, dz))
        for dm in range(ms):
            if dz == 0 and dm == 0:
                continue
            sources.append((dz, dm))
            arrived.append(piece if dm == 0 else lax.ppermute(piece, "mode", swap_pairs(ms, dm)))
    object_out = call(
        functools.partial(spectral_kernel, sources=tuple(sources), sizes=(zs, ms)),
        (spectra_basis, analysis, threshold, object_new, *arrived),
        3,
        shape(object_field.shape, f32),
        name="spectral",
    )
    for distance in [1 << k for k in range(1, tiles.bit_length() - 1)]:
        other = lax.ppermute(share, "tile", swap_pairs(tiles, distance))
        share = (share.astype(f32) + other.astype(f32)).astype(bf16)
    other = lax.ppermute(share, "tile", swap_pairs(tiles, 1))
    probe_out = call(
        probe_kernel, (probe_field, share, other), 0, shape(probe_field.shape, f32), name="probes"
    )
    return (object_out, probe_out)


def solution(mesh):
    placed = (
        P(None, ("groups", "energy", "mode"), "tile", None),
        P(None, None, ("groups", "energy", "mode"), None, None),
        P(("groups", "energy", "mode"), "tile", None, None),
        P(("groups", "tile"), None),
        P(),
        P(),
        P(),
    )
    return jax.shard_map(
        body,
        mesh=mesh,
        in_specs=placed,
        out_specs=(
            P(None, ("groups", "energy", "mode"), "tile", None),
            P(None, None, ("groups", "energy", "mode"), None, None),
        ),
        check_vma=False,
    )
```

```python
import functools
import math

import jax
import jax.numpy as jnp
import ml_dtypes
import numpy as np
from jax import lax
from jax.experimental import pallas as pl
from jax.experimental.pallas import tpu as pltpu
from jax.sharding import PartitionSpec as P

PCOLS = 2
STEP = 32
LANES = 128
PAD_ROWS = 16

VMEM = pl.BlockSpec(memory_space=pltpu.VMEM)
SMEM = pl.BlockSpec(memory_space=pltpu.SMEM)


def swap_pairs(size, distance):
    return [(i, i ^ distance) for i in range(size)]


def dft_tables(extent):
    counter = np.arange(extent)
    phases = -2.0 * math.pi / extent * (counter[:, None] * counter[None, :] % extent)
    cosine = np.cos(phases) / math.sqrt(extent)
    sine = np.sin(phases) / math.sqrt(extent)
    forward = np.block([[cosine, -sine], [sine, cosine]])
    backward = np.block([[cosine, sine], [-sine, cosine]])
    return (
        jnp.asarray(forward.astype(np.float32).astype(ml_dtypes.bfloat16)),
        jnp.asarray(backward.astype(np.float32).astype(ml_dtypes.bfloat16)),
    )


def corner(offsets, q):
    row = STEP * (q // PCOLS) + offsets[0, q]
    col = STEP * (q % PCOLS) + offsets[1, q]
    return row, col


def spread(block, row):
    lane = lax.broadcasted_iota(jnp.int32, block.shape, 1)
    turned = pltpu.roll(block, row, 1)
    left = jnp.where(lane >= row, turned, 0.0)
    right = jnp.where(lane < row, turned, 0.0)
    return left, right


def round_kernel(offsets_ref, object_ref, message_ref):
    cols, rows = object_ref.shape[2:]
    positions = offsets_ref.shape[1]
    for part in range(2):
        message_ref[part, :cols] = object_ref[part, 0].astype(jnp.bfloat16)
    lane = lax.broadcasted_iota(jnp.int32, (PAD_ROWS, rows), 1)
    line = jnp.zeros((PAD_ROWS, rows), jnp.float32)
    for k in range(2):
        for q in range(positions):
            value = offsets_ref[k, q].astype(jnp.float32)
            line = jnp.where(lane == k * positions + q, value, line)
    for part in range(2):
        message_ref[part, cols:] = line.astype(jnp.bfloat16)


def turn_kernel(probe_ref, moduli_ref, turned_ref, moduli_out_ref):
    modes = probe_ref.shape[1]
    for part in range(2):
        for m in range(modes):
            turned_ref[part, m] = probe_ref[part, m, 0].T
    for q in range(moduli_ref.shape[1]):
        moduli_out_ref[q] = moduli_ref[0, q].astype(jnp.float32).T


def wave_kernel(
    offsets_ref,
    own_ref,
    below_ref,
    probe_ref,
    moduli_ref,
    forward_ref,
    backward_ref,
    upper_ref,
    lower_ref,
    share_ref,
    extended,
    total,
    window,
    stacked,
    tall,
    long,
    probe_num,
    probe_den,
    *,
    tiles,
    group,
):
    extent = probe_ref.shape[-1]
    modes = probe_ref.shape[1]
    cols = own_ref.shape[1] - PAD_ROWS
    positions = offsets_ref.shape[1]
    has_below = lax.axis_index("tile") < tiles - 1
    for part in range(2):
        extended[part, 0] = own_ref[part, :cols].astype(jnp.float32)
        below = below_ref[part, :cols].astype(jnp.float32)
        extended[part, 1] = jnp.where(has_below, below, 0.0)
    total[...] = jnp.zeros_like(total)
    probe_num[...] = jnp.zeros_like(probe_num)
    probe_den[...] = jnp.zeros_like(probe_den)
    lane = lax.broadcasted_iota(jnp.int32, (extent, extent), 1)

    def places(member, m):
        w = member * modes + m
        return slice(w * extent, (w + 1) * extent)

    def step(block, carry):
        for member in range(group):
            q = block * group + member
            row, col = corner(offsets_ref, q)
            here = pl.ds(col, extent)
            for part in range(2):
                left = pltpu.roll(extended[part, 0, here], extent - row, 1)
                right = pltpu.roll(extended[part, 1, here], extent - row, 1)
                window[member, part] = jnp.where(lane < extent - row, left, right)
            object_real = window[member, 0]
            object_imag = window[member, 1]
            probe_den[...] += object_real * object_real + object_imag * object_imag
            for m in range(modes):
                place = places(member, m)
                probe_real = probe_ref[0, m]
                probe_imag = probe_ref[1, m]
                wave_real = probe_real * object_real - probe_imag * object_imag
                wave_imag = probe_real * object_imag + probe_imag * object_real
                stacked[0, place] = wave_real
                stacked[1, place] = wave_imag
                tall[place, :extent] = wave_real.astype(jnp.bfloat16)
                tall[place, extent:] = wave_imag.astype(jnp.bfloat16)
        halfway = jnp.dot(tall[...], backward_ref[...], preferred_element_type=jnp.float32)
        for member in range(group):
            for m in range(modes):
                place = places(member, m)
                long[:extent, place] = halfway[place, :extent].astype(jnp.bfloat16)
                long[extent:, place] = halfway[place, extent:].astype(jnp.bfloat16)
        spectrum = jnp.dot(forward_ref[...], long[...], preferred_element_type=jnp.float32)
        for member in range(group):
            q = block * group + member
            magnitude = jnp.full((extent, extent), 0.01, jnp.float32)
            for m in range(modes):
                place = places(member, m)
                real = spectrum[:extent, place]
                imag = spectrum[extent:, place]
                magnitude += real * real + imag * imag
            factor = moduli_ref[q] * lax.rsqrt(magnitude)
            for m in range(modes):
                place = places(member, m)
                long[:extent, place] = (spectrum[:extent, place] * factor).astype(jnp.bfloat16)
                long[extent:, place] = (spectrum[extent:, place] * factor).astype(jnp.bfloat16)
        returned = jnp.dot(backward_ref[...], long[...], preferred_element_type=jnp.float32)
        for member in range(group):
            for m in range(modes):
                place = places(member, m)
                tall[place, :extent] = returned[:extent, place].astype(jnp.bfloat16)
                tall[place, extent:] = returned[extent:, place].astype(jnp.bfloat16)
        new_wave = jnp.dot(tall[...], forward_ref[...], preferred_element_type=jnp.float32)
        for member in range(group):
            q = block * group + member
            row, col = corner(offsets_ref, q)
            here = pl.ds(col, extent)
            object_real = window[member, 0]
            object_imag = window[member, 1]
            sum_real = jnp.zeros((extent, extent), jnp.float32)
            sum_imag = jnp.zeros((extent, extent), jnp.float32)
            for m in range(modes):
                place = places(member, m)
                change_real = new_wave[place, :extent] - stacked[0, place]
                change_imag = new_wave[place, extent:] - stacked[1, place]
                probe_real = probe_ref[0, m]
                probe_imag = probe_ref[1, m]
                sum_real += probe_real * change_real + probe_imag * change_imag
                sum_imag += probe_real * change_imag - probe_imag * change_real
                probe_num[0, m] += object_real * change_real + object_imag * change_imag
                probe_num[1, m] += object_real * change_imag - object_imag * change_real
            for part, value in enumerate((sum_real, sum_imag)):
                for side, moved in enumerate(spread(value, row)):
                    total[part, side, here] += moved
        return carry

    lax.fori_loop(0, positions // group, step, 0)
    for part in range(2):
        upper_ref[part] = total[part, 0]
        lower_ref[part] = total[part, 1].astype(jnp.bfloat16)
        for m in range(modes):
            share_ref[part * modes + m] = probe_num[part, m].astype(jnp.bfloat16)
    share_ref[2 * modes] = probe_den[...].astype(jnp.bfloat16)


def weight_kernel(offsets_ref, above_ref, probe_ref, inverse_ref, own, other):
    extent = probe_ref.shape[-1]
    modes = probe_ref.shape[1]
    cols = inverse_ref.shape[0]
    positions = offsets_ref.shape[1]
    power = jnp.zeros((extent, extent), jnp.float32)
    for part in range(2):
        for m in range(modes):
            value = probe_ref[part, m]
            power += value * value
    largest = jnp.max(power)
    own[...] = jnp.zeros_like(own)
    other[...] = jnp.zeros_like(other)
    line = above_ref[0, cols : cols + PAD_ROWS].astype(jnp.float32)[:8]
    lane = lax.broadcasted_iota(jnp.int32, line.shape, 1)
    for q in range(positions):
        row, col = corner(offsets_ref, q)
        left, unused = spread(power, row)
        own[pl.ds(col, extent)] += left
        above = [
            jnp.max(jnp.where(lane == k * positions + q, line, 0.0)).astype(jnp.int32) for k in range(2)
        ]
        row = STEP * (q // PCOLS) + above[0]
        col = STEP * (q % PCOLS) + above[1]
        unused, right = spread(power, row)
        other[pl.ds(col, extent)] += right
    has_above = lax.axis_index("tile") > 0
    weight = own[...] + jnp.where(has_above, other[...], 0.0)
    inverse_ref[...] = 1.0 / (weight + 0.1 * largest + 1e-06)


def object_kernel(object_ref, upper_ref, received_ref, inverse_ref, new_ref, sent_ref):
    has_above = lax.axis_index("tile") > 0
    for part in range(2):
        received = received_ref[part].astype(jnp.float32)
        wave = upper_ref[part] + jnp.where(has_above, received, 0.0)
        value = object_ref[part, 0] + wave * inverse_ref[...]
        new_ref[part] = value
        sent_ref[part] = value.astype(jnp.bfloat16)


def spectral_kernel(basis_ref, analysis_ref, threshold_ref, own_ref, *refs, sources, sizes):
    others, out_ref = refs[:-1], refs[-1]
    parts, rows, unused = own_ref.shape
    components = threshold_ref.shape[0]
    zs, ms = sizes
    z = lax.axis_index("energy")
    m = lax.axis_index("mode")
    mine = z * ms + m
    labels = [(z ^ dz) * ms + (m ^ dm) for dz, dm in sources]
    chunk = 32
    per_part = rows // chunk

    def step(index, carry):
        part = index // per_part
        here = pl.ds(pl.multiple_of((index % per_part) * chunk, chunk), chunk)
        own = own_ref[part, here]
        values = [own] + [ref[part, here].astype(jnp.float32) for ref in others]
        projected = 0.5 * own
        for k in range(components):
            c = analysis_ref[k, mine] * values[0]
            for label, value in zip(labels, values[1:]):
                c += analysis_ref[k, label] * value
            t = threshold_ref[k]
            c = c - jnp.minimum(jnp.maximum(c, -t), t)
            projected += (0.5 * basis_ref[mine, k]) * c
        out_ref[part, 0, here] = projected
        return carry

    lax.fori_loop(0, parts * per_part, step, 0)


def probe_kernel(probe_ref, own_ref, received_ref, out_ref):
    modes = probe_ref.shape[1]
    density = own_ref[2 * modes].astype(jnp.float32) + received_ref[2 * modes].astype(jnp.float32)
    inverse = 1.0 / (density + 0.1 * jnp.max(density) + 1e-06)
    for part in range(2):
        for m in range(modes):
            k = part * modes + m
            numerator = own_ref[k].astype(jnp.float32) + received_ref[k].astype(jnp.float32)
            out_ref[part, m, 0] = probe_ref[part, m, 0] + (numerator * inverse).T


def call(kernel, inputs, scalars, outputs, scratch=(), limit=4, name=None):
    return pl.pallas_call(
        kernel,
        out_shape=outputs,
        in_specs=[SMEM] * scalars + [VMEM] * (len(inputs) - scalars),
        out_specs=jax.tree.map(lambda _: VMEM, outputs),
        scratch_shapes=list(scratch),
        compiler_params=pltpu.CompilerParams(vmem_limit_bytes=limit << 20),
        name=name,
    )(*inputs)


def body(object_field, probe_field, modulus, offsets, spectra_basis, analysis, threshold):
    extent = probe_field.shape[-1]
    modes = probe_field.shape[1]
    object_field = jnp.transpose(object_field, (0, 1, 3, 2))
    offsets = jnp.transpose(offsets)
    cols, rows = object_field.shape[2:]
    positions = offsets.shape[1]
    tiles = lax.axis_size("tile")
    zs = lax.axis_size("energy")
    ms = lax.axis_size("mode")
    forward, backward = dft_tables(extent)
    shape = jax.ShapeDtypeStruct
    f32, bf16 = jnp.float32, jnp.bfloat16

    message = call(
        round_kernel, (offsets, object_field), 1, shape((2, cols + PAD_ROWS, rows), bf16), name="round"
    )
    if tiles == 2:
        below = above = lax.ppermute(message, "tile", swap_pairs(2, 1))
    else:
        below = lax.ppermute(message, "tile", [(i + 1, i) for i in range(tiles - 1)])
        above = lax.ppermute(message, "tile", [(i, i + 1) for i in range(tiles - 1)])
    turned, moduli = call(
        turn_kernel,
        (probe_field, modulus),
        0,
        (shape((2, modes, extent, extent), f32), shape((positions, extent, extent), f32)),
        name="turn",
    )

    group = 2
    waves = group * modes
    upper, lower, share = call(
        functools.partial(wave_kernel, tiles=tiles, group=group),
        (offsets, message, below, turned, moduli, forward, backward),
        1,
        (
            shape((2, cols, rows), f32),
            shape((2, cols, rows), bf16),
            shape((2 * modes + 1, extent, extent), bf16),
        ),
        (
            pltpu.VMEM((2, 2, cols, LANES), f32),
            pltpu.VMEM((2, 2, cols, LANES), f32),
            pltpu.VMEM((group, 2, extent, extent), f32),
            pltpu.VMEM((2, waves * extent, extent), f32),
            pltpu.VMEM((waves * extent, 2 * extent), bf16),
            pltpu.VMEM((2 * extent, waves * extent), bf16),
            pltpu.VMEM((2, modes, extent, extent), f32),
            pltpu.VMEM((extent, extent), f32),
        ),
        limit=20,
        name="wave",
    )
    if tiles == 2:
        received = lax.ppermute(lower, "tile", swap_pairs(2, 1))
    else:
        received = lax.ppermute(lower, "tile", [(i, i + 1) for i in range(tiles - 1)])
    inverse = call(
        weight_kernel,
        (offsets, above, turned),
        1,
        shape((cols, rows), f32),
        (pltpu.VMEM((cols, LANES), f32), pltpu.VMEM((cols, LANES), f32)),
        name="weight",
    )
    object_new, sent = call(
        object_kernel,
        (object_field, upper, received, inverse),
        0,
        (shape((2, cols, rows), f32), shape((2, cols, rows), bf16)),
        name="object",
    )
    sources = []
    arrived = []
    for dz in range(zs):
        piece = sent if dz == 0 else lax.ppermute(sent, "energy", swap_pairs(zs, dz))
        for dm in range(ms):
            if dz == 0 and dm == 0:
                continue
            sources.append((dz, dm))
            arrived.append(piece if dm == 0 else lax.ppermute(piece, "mode", swap_pairs(ms, dm)))
    object_out = call(
        functools.partial(spectral_kernel, sources=tuple(sources), sizes=(zs, ms)),
        (spectra_basis, analysis, threshold, object_new, *arrived),
        3,
        shape(object_field.shape, f32),
        name="spectral",
    )
    for distance in [1 << k for k in range(1, tiles.bit_length() - 1)]:
        other = lax.ppermute(share, "tile", swap_pairs(tiles, distance))
        share = (share.astype(f32) + other.astype(f32)).astype(bf16)
    other = lax.ppermute(share, "tile", swap_pairs(tiles, 1))
    probe_out = call(
        probe_kernel, (probe_field, share, other), 0, shape(probe_field.shape, f32), name="probes"
    )
    return (jnp.transpose(object_out, (0, 1, 3, 2)), probe_out)


def solution(mesh):
    placed = (
        P(None, ("groups", "energy", "mode"), "tile", None),
        P(None, None, ("groups", "energy", "mode"), None, None),
        P(("groups", "energy", "mode"), "tile", None, None),
        P(("groups", "tile"), None),
        P(),
        P(),
        P(),
    )
    return jax.shard_map(
        body,
        mesh=mesh,
        in_specs=placed,
        out_specs=(
            P(None, ("groups", "energy", "mode"), "tile", None),
            P(None, None, ("groups", "energy", "mode"), None, None),
        ),
        check_vma=False,
    )
```

```python
import functools
import math

import jax
import jax.numpy as jnp
import ml_dtypes
import numpy as np
from jax import lax
from jax.experimental import pallas as pl
from jax.experimental.pallas import tpu as pltpu
from jax.sharding import PartitionSpec as P

PCOLS = 2
STEP = 32
LANES = 128
PAD_ROWS = 16


def swap_pairs(size, distance):
    return [(i, i ^ distance) for i in range(size)]


def dft_tables(extent):
    counter = np.arange(extent)
    phases = -2.0 * math.pi / extent * (counter[:, None] * counter[None, :] % extent)
    cosine = np.cos(phases) / math.sqrt(extent)
    sine = np.sin(phases) / math.sqrt(extent)
    forward = np.block([[cosine, -sine], [sine, cosine]])
    backward = np.block([[cosine, sine], [-sine, cosine]])
    return (
        jnp.asarray(forward.astype(np.float32).astype(ml_dtypes.bfloat16)),
        jnp.asarray(backward.astype(np.float32).astype(ml_dtypes.bfloat16)),
    )


def corner(offsets, q):
    row = STEP * (q // PCOLS) + offsets[0, q]
    col = STEP * (q % PCOLS) + offsets[1, q]
    return row, col


def spread(block, row):
    lane = lax.broadcasted_iota(jnp.int32, block.shape, 1)
    turned = pltpu.roll(block, row, 1)
    left = jnp.where(lane >= row, turned, 0.0)
    right = jnp.where(lane < row, turned, 0.0)
    return left, right


def round_kernel(offsets_hbm, object_hbm, message_ref, object_ref, offsets_ref, sems):
    cols, rows = object_ref.shape[1:]
    positions = offsets_ref.shape[1]
    copies = [pltpu.make_async_copy(offsets_hbm, offsets_ref, sems.at[2])]
    copies += [
        pltpu.make_async_copy(object_hbm.at[part, 0], object_ref.at[part], sems.at[part])
        for part in range(2)
    ]
    for copy in copies:
        copy.start()
    copies[0].wait()
    lane = lax.broadcasted_iota(jnp.int32, (PAD_ROWS, rows), 1)
    line = jnp.zeros((PAD_ROWS, rows), jnp.float32)
    for k in range(2):
        for q in range(positions):
            value = offsets_ref[k, q].astype(jnp.float32)
            line = jnp.where(lane == k * positions + q, value, line)
    for part in range(2):
        copies[1 + part].wait()
        message_ref[part, :cols] = object_ref[part].astype(jnp.bfloat16)
        message_ref[part, cols:] = line.astype(jnp.bfloat16)


def turn_kernel(
    offsets_hbm,
    analysis_hbm,
    basis_hbm,
    threshold_hbm,
    forward_hbm,
    backward_hbm,
    probe_hbm,
    moduli_hbm,
    offsets_out_ref,
    forward_ref,
    backward_ref,
    turned_ref,
    moduli_out_ref,
    power_ref,
    weight_ref,
    analysis_table_ref,
    last_table_ref,
    offsets_ref,
    analysis_ref,
    basis_ref,
    threshold_ref,
    probe_ref,
    moduli_ref,
    sems,
    *,
    sources,
    sizes,
):
    modes = probe_ref.shape[1]
    extent = probe_ref.shape[-1]
    positions = offsets_ref.shape[1]
    pairs = [
        (offsets_hbm, offsets_ref),
        (probe_hbm, probe_ref),
        (moduli_hbm, moduli_ref),
        (analysis_hbm, analysis_ref),
        (basis_hbm, basis_ref),
        (threshold_hbm, threshold_ref),
        (forward_hbm, forward_ref),
        (backward_hbm, backward_ref),
        (offsets_hbm, offsets_out_ref),
    ]
    copies = [
        pltpu.make_async_copy(source, target, sems.at[k])
        for k, (source, target) in enumerate(pairs)
    ]
    for copy in copies:
        copy.start()
    for copy in copies[3:6]:
        copy.wait()
    _, ms = sizes
    z = lax.axis_index("energy")
    m = lax.axis_index("mode")
    tile = analysis_table_ref.shape[2:]
    for k in range(threshold_ref.shape[0]):
        for number, (dz, dm) in enumerate(sources):
            label = (z ^ dz) * ms + (m ^ dm)
            analysis_table_ref[number, k] = jnp.full(tile, analysis_ref[k, label])
        last_table_ref[0, k] = jnp.full(tile, 0.5 * basis_ref[z * ms + m, k])
        last_table_ref[1, k] = jnp.full(tile, threshold_ref[k])
    copies[0].wait()
    copies[1].wait()
    power = jnp.zeros((extent, extent), jnp.float32)
    for part in range(2):
        for m in range(modes):
            value = probe_ref[part, m, 0].T
            turned_ref[part, m] = value
            power += value * value
    power_ref[...] = power
    weight_ref[...] = jnp.full_like(weight_ref, 0.1 * jnp.max(power) + 1e-06)
    for q in range(positions):
        row, col = corner(offsets_ref, q)
        left, _ = spread(power, row)
        weight_ref[pl.ds(col, extent)] += left
    copies[2].wait()
    for q in range(positions):
        moduli_out_ref[q] = moduli_ref[0, q].astype(jnp.float32).T
    for copy in copies[6:]:
        copy.wait()


def cut(extended, offsets_ref, q, extent):
    row, col = corner(offsets_ref, q)
    here = pl.ds(col, extent)
    lane = lax.broadcasted_iota(jnp.int32, (extent, extent), 1)
    found = []
    for part in range(2):
        left = pltpu.roll(extended[part, 0, here], extent - row, 1)
        right = pltpu.roll(extended[part, 1, here], extent - row, 1)
        found.append(jnp.where(lane < extent - row, left, right))
    return found


def extend(extended, own_ref, below_ref, tiles):
    cols = extended.shape[2]
    has_below = lax.axis_index("tile") < tiles - 1
    for part in range(2):
        extended[part, 0] = own_ref[part, :cols].astype(jnp.float32)
        below = below_ref[part, :cols].astype(jnp.float32)
        extended[part, 1] = jnp.where(has_below, below, 0.0)


def side_by_side(blocks):
    return jnp.concatenate(blocks, axis=1)


def stack_up(blocks):
    return jnp.concatenate(blocks, axis=0)


def wave_kernel(
    offsets_ref,
    own_ref,
    below_ref,
    probe_ref,
    moduli_ref,
    forward_ref,
    backward_ref,
    upper_ref,
    lower_ref,
    change_ref,
    extended,
    total,
    *,
    tiles,
    group,
):
    extent = probe_ref.shape[-1]
    modes = probe_ref.shape[1]
    positions = offsets_ref.shape[1]
    waves = group * modes
    extend(extended, own_ref, below_ref, tiles)
    total[...] = jnp.zeros_like(total)
    low = slice(0, extent)
    high = slice(extent, 2 * extent)

    def dot(left, right):
        return jnp.dot(left, right, preferred_element_type=jnp.float32)

    def span(w):
        return slice(w * extent, (w + 1) * extent)

    for block in range(positions // group):
        rounded = []
        for member in range(group):
            q = block * group + member
            object_real, object_imag = cut(extended, offsets_ref, q, extent)
            for m in range(modes):
                probe_real = probe_ref[0, m]
                probe_imag = probe_ref[1, m]
                wave_real = probe_real * object_real - probe_imag * object_imag
                wave_imag = probe_real * object_imag + probe_imag * object_real
                change_ref[q, m, 0] = wave_real
                change_ref[q, m, 1] = wave_imag
                rounded.append(side_by_side([wave_real, wave_imag]).astype(jnp.bfloat16))
        halfway = dot(stack_up(rounded), backward_ref[...]).astype(jnp.bfloat16)
        standing = side_by_side(
            [stack_up([halfway[span(w), low], halfway[span(w), high]]) for w in range(waves)]
        )
        spectrum = dot(forward_ref[...], standing)
        scaled = []
        for member in range(group):
            q = block * group + member
            magnitude = jnp.full((extent, extent), 0.01, jnp.float32)
            for m in range(modes):
                place = span(member * modes + m)
                real = spectrum[low, place]
                imag = spectrum[high, place]
                magnitude += real * real + imag * imag
            factor = moduli_ref[q] * lax.rsqrt(magnitude)
            for m in range(modes):
                place = span(member * modes + m)
                scaled.append(
                    stack_up([spectrum[low, place] * factor, spectrum[high, place] * factor]).astype(
                        jnp.bfloat16
                    )
                )
        returned = dot(backward_ref[...], side_by_side(scaled)).astype(jnp.bfloat16)
        lying = stack_up(
            [side_by_side([returned[low, span(w)], returned[high, span(w)]]) for w in range(waves)]
        )
        new_wave = dot(lying, forward_ref[...])
        for member in range(group):
            q = block * group + member
            row, col = corner(offsets_ref, q)
            here = pl.ds(col, extent)
            sum_real = jnp.zeros((extent, extent), jnp.float32)
            sum_imag = jnp.zeros((extent, extent), jnp.float32)
            for m in range(modes):
                place = span(member * modes + m)
                change_real = new_wave[place, low] - change_ref[q, m, 0]
                change_imag = new_wave[place, high] - change_ref[q, m, 1]
                change_ref[q, m, 0] = change_real
                change_ref[q, m, 1] = change_imag
                probe_real = probe_ref[0, m]
                probe_imag = probe_ref[1, m]
                sum_real += probe_real * change_real + probe_imag * change_imag
                sum_imag += probe_real * change_imag - probe_imag * change_real
            for part, value in enumerate((sum_real, sum_imag)):
                for side, moved in enumerate(spread(value, row)):
                    total[part, side, here] += moved

    for part in range(2):
        upper_ref[part] = total[part, 0]
        lower_ref[part] = total[part, 1].astype(jnp.bfloat16)


def share_kernel(
    offsets_ref, own_ref, below_ref, change_ref, share_ref, extended, window, *, tiles
):
    extent = change_ref.shape[-1]
    positions, modes = change_ref.shape[:2]
    extend(extended, own_ref, below_ref, tiles)
    density = jnp.zeros((extent, extent), jnp.float32)
    for q in range(positions):
        object_real, object_imag = cut(extended, offsets_ref, q, extent)
        window[q, 0] = object_real
        window[q, 1] = object_imag
        density += object_real * object_real + object_imag * object_imag
    share_ref[2 * modes] = density.astype(jnp.bfloat16)
    chunk = 16

    def step(index, carry):
        here = pl.ds(pl.multiple_of(index * chunk, chunk), chunk)
        for m in range(modes):
            sum_real = jnp.zeros((chunk, extent), jnp.float32)
            sum_imag = jnp.zeros((chunk, extent), jnp.float32)
            for q in range(positions):
                object_real = window[q, 0, here]
                object_imag = window[q, 1, here]
                change_real = change_ref[q, m, 0, here]
                change_imag = change_ref[q, m, 1, here]
                sum_real += object_real * change_real + object_imag * change_imag
                sum_imag += object_real * change_imag - object_imag * change_real
            share_ref[m, here] = sum_real.astype(jnp.bfloat16)
            share_ref[modes + m, here] = sum_imag.astype(jnp.bfloat16)
        return carry

    lax.fori_loop(0, extent // chunk, step, 0)


def weight_kernel(above_ref, power_ref, weight_ref, inverse_ref, other, *, positions):
    extent = power_ref.shape[-1]
    cols = inverse_ref.shape[0]
    power = power_ref[...]
    other[...] = jnp.zeros_like(other)
    line = above_ref[0, cols : cols + PAD_ROWS].astype(jnp.float32)[:8]
    lane = lax.broadcasted_iota(jnp.int32, line.shape, 1)
    for q in range(positions):
        above = [
            jnp.max(jnp.where(lane == k * positions + q, line, 0.0)).astype(jnp.int32) for k in range(2)
        ]
        row = STEP * (q // PCOLS) + above[0]
        col = STEP * (q % PCOLS) + above[1]
        _, right = spread(power, row)
        other[pl.ds(col, extent)] += right
    has_above = lax.axis_index("tile") > 0
    inverse_ref[...] = 1.0 / (weight_ref[...] + jnp.where(has_above, other[...], 0.0))


def object_kernel(object_ref, upper_ref, received_ref, inverse_ref, new_ref, sent_ref):
    has_above = lax.axis_index("tile") > 0
    for part in range(2):
        received = received_ref[part].astype(jnp.float32)
        wave = upper_ref[part] + jnp.where(has_above, received, 0.0)
        value = object_ref[part] + wave * inverse_ref[...]
        new_ref[part] = value
        sent_ref[part] = value.astype(jnp.bfloat16)


def mix_kernel(table_ref, *refs, first, chained, chunk):
    mixed_ref = refs[-1]
    refs = refs[:-1]
    before, refs = (refs[0], refs[1:]) if chained else (None, refs)
    components, parts, rows, lanes = mixed_ref.shape
    per_part = rows // chunk
    height = table_ref.shape[2]

    def step(index, carry):
        part = index // per_part
        here = pl.ds(pl.multiple_of((index % per_part) * chunk, chunk), chunk)
        folded = (chunk // height, height, lanes)
        values = [ref[part, here].astype(jnp.float32).reshape(folded) for ref in refs]
        for k in range(components):
            terms = [table_ref[first + n, k] * value for n, value in enumerate(values)]
            if before is not None:
                terms.insert(0, before[k, part, here].reshape(folded))
            mixed_ref[k, part, here] = functools.reduce(jnp.add, terms).reshape(chunk, lanes)
        return carry

    lax.fori_loop(0, parts * per_part, step, 0)


def spectral_kernel(table_ref, last_ref, own_ref, mixed_ref, *refs, first, chunk):
    refs, out_ref = refs[:-1], refs[-1]
    parts, rows, lanes = own_ref.shape
    components = last_ref.shape[1]
    per_part = rows // chunk
    height = table_ref.shape[2]

    def step(index, carry):
        part = index // per_part
        here = pl.ds(pl.multiple_of((index % per_part) * chunk, chunk), chunk)
        folded = (chunk // height, height, lanes)
        values = [ref[part, here].astype(jnp.float32).reshape(folded) for ref in refs]
        terms = [0.5 * own_ref[part, here].reshape(folded)]
        for k in range(components):
            c = mixed_ref[k, part, here].reshape(folded)
            for n, value in enumerate(values):
                c += table_ref[first + n, k] * value
            t = last_ref[1, k]
            c = c - jnp.minimum(jnp.maximum(c, -t), t)
            terms.append(last_ref[0, k] * c)
        while len(terms) > 1:
            terms = [sum(terms[k : k + 2][1:], terms[k]) for k in range(0, len(terms), 2)]
        out_ref[part, 0, here] = terms[0].reshape(chunk, lanes)
        return carry

    lax.fori_loop(0, parts * per_part, step, 0)


def probe_kernel(probe_ref, own_ref, received_ref, out_ref):
    modes = probe_ref.shape[1]
    density = own_ref[2 * modes].astype(jnp.float32) + received_ref[2 * modes].astype(jnp.float32)
    inverse = 1.0 / (density + 0.1 * jnp.max(density) + 1e-06)
    for part in range(2):
        for m in range(modes):
            k = part * modes + m
            numerator = own_ref[k].astype(jnp.float32) + received_ref[k].astype(jnp.float32)
            out_ref[part, m, 0] = (probe_ref[part, m] + numerator * inverse).T


def call(kernel, inputs, places, outputs, scratch=(), limit=4):
    inputs = [
        pltpu.with_memory_space_constraint(x, pltpu.HBM) if p == "h" else x
        for x, p in zip(inputs, places)
    ]
    kinds = {"s": pltpu.SMEM, "v": pltpu.VMEM, "h": pltpu.HBM}
    return pl.pallas_call(
        kernel,
        out_shape=outputs,
        in_specs=[pl.BlockSpec(memory_space=kinds[p]) for p in places],
        out_specs=jax.tree.map(lambda _: pl.BlockSpec(memory_space=pltpu.VMEM), outputs),
        scratch_shapes=list(scratch),
        compiler_params=pltpu.CompilerParams(vmem_limit_bytes=limit << 20),
    )(*inputs)


def body(object_field, probe_field, modulus, offsets, spectra_basis, analysis, threshold):
    extent = probe_field.shape[-1]
    modes = probe_field.shape[1]
    object_field = jnp.transpose(object_field, (0, 1, 3, 2))
    offsets = jnp.transpose(offsets)
    cols, rows = object_field.shape[2:]
    positions = offsets.shape[1]
    tiles = lax.axis_size("tile")
    zs = lax.axis_size("energy")
    ms = lax.axis_size("mode")
    forward, backward = dft_tables(extent)
    shape = jax.ShapeDtypeStruct
    f32, bf16 = jnp.float32, jnp.bfloat16

    message, object_here = call(
        round_kernel,
        (offsets, object_field),
        "hh",
        (shape((2, cols + PAD_ROWS, rows), bf16), shape((2, cols, rows), f32)),
        (pltpu.SMEM((2, positions), jnp.int32), pltpu.SemaphoreType.DMA((3,))),
    )
    if tiles == 2:
        below = above = lax.ppermute(message, "tile", swap_pairs(2, 1))
    else:
        below = lax.ppermute(message, "tile", [(i + 1, i) for i in range(tiles - 1)])
        above = lax.ppermute(message, "tile", [(i, i + 1) for i in range(tiles - 1)])

    far = zs // 2
    stages = [
        [(dz, dm) for dz in (0, 1) for dm in range(ms)],
        [(dz, dm) for dz in range(2, zs) for dm in range(ms) if dz != far] + [(far, 0)],
        [(far, dm) for dm in range(1, ms)],
    ]
    sources = sum(stages, [])
    components = threshold.shape[0]
    offsets, forward, backward, turned, moduli, power, weight, table, last_table = call(
        functools.partial(turn_kernel, sources=tuple(sources), sizes=(zs, ms)),
        (offsets, analysis, spectra_basis, threshold, forward, backward, probe_field, modulus),
        "hhhhhhhh",
        (
            shape((2, positions), jnp.int32),
            shape(forward.shape, bf16),
            shape(backward.shape, bf16),
            shape((2, modes, extent, extent), f32),
            shape((positions, extent, extent), f32),
            shape((extent, extent), f32),
            shape((cols, rows), f32),
            shape((len(sources), components, 8, LANES), f32),
            shape((2, components, 8, LANES), f32),
        ),
        (
            pltpu.SMEM((2, positions), jnp.int32),
            pltpu.SMEM(analysis.shape, f32),
            pltpu.SMEM(spectra_basis.shape, f32),
            pltpu.SMEM(threshold.shape, f32),
            pltpu.VMEM(probe_field.shape, f32),
            pltpu.VMEM(modulus.shape, bf16),
            pltpu.SemaphoreType.DMA((9,)),
        ),
        limit=8,
    )
    upper, lower, change = call(
        functools.partial(wave_kernel, tiles=tiles, group=2),
        (offsets, message, below, turned, moduli, forward, backward),
        "svvvvvv",
        (
            shape((2, cols, rows), f32),
            shape((2, cols, rows), bf16),
            shape((positions, modes, 2, extent, extent), f32),
        ),
        (
            pltpu.VMEM((2, 2, cols, LANES), f32),
            pltpu.VMEM((2, 2, cols, LANES), f32),
        ),
        limit=24,
    )
    if tiles == 2:
        received = lax.ppermute(lower, "tile", swap_pairs(2, 1))
    else:
        received = lax.ppermute(lower, "tile", [(i, i + 1) for i in range(tiles - 1)])
    inverse = call(
        functools.partial(weight_kernel, positions=positions),
        (above, power, weight),
        "vvv",
        shape((cols, rows), f32),
        (pltpu.VMEM((cols, rows), f32),),
    )
    share = call(
        functools.partial(share_kernel, tiles=tiles),
        (offsets, message, below, change),
        "svvv",
        shape((2 * modes + 1, extent, extent), bf16),
        (
            pltpu.VMEM((2, 2, cols, LANES), f32),
            pltpu.VMEM((positions, 2, extent, extent), f32),
        ),
        limit=8,
    )
    object_new, sent = call(
        object_kernel,
        (object_here, upper, received, inverse),
        "vvvv",
        (shape((2, cols, rows), f32), shape((2, cols, rows), bf16)),
    )
    pieces = {(0, 0): sent}
    for dz in range(1, zs):
        pieces[dz, 0] = lax.ppermute(sent, "energy", swap_pairs(zs, dz))
    for dz in range(zs):
        for dm in range(1, ms):
            pieces[dz, dm] = lax.ppermute(pieces[dz, 0], "mode", swap_pairs(ms, dm))
    mixed = None
    first = 0
    for stage in stages[:2]:
        inputs = [table] + ([] if mixed is None else [mixed]) + [pieces[s] for s in stage]
        mixed = call(
            functools.partial(mix_kernel, first=first, chained=mixed is not None, chunk=64),
            inputs,
            "v" * len(inputs),
            shape((components, 2, cols, rows), f32),
        )
        first += len(stage)
    inputs = [table, last_table, object_new, mixed] + [pieces[s] for s in stages[2]]
    object_out = call(
        functools.partial(spectral_kernel, first=first, chunk=64),
        inputs,
        "v" * len(inputs),
        shape(object_field.shape, f32),
    )
    for distance in [1 << k for k in range(1, tiles.bit_length() - 1)]:
        other = lax.ppermute(share, "tile", swap_pairs(tiles, distance))
        share = (share.astype(f32) + other.astype(f32)).astype(bf16)
    other = lax.ppermute(share, "tile", swap_pairs(tiles, 1))
    probe_out = call(probe_kernel, (turned, share, other), "vvv", shape(probe_field.shape, f32))
    return (jnp.transpose(object_out, (0, 1, 3, 2)), probe_out)


def solution(mesh):
    placed = (
        P(None, ("groups", "energy", "mode"), "tile", None),
        P(None, None, ("groups", "energy", "mode"), None, None),
        P(("groups", "energy", "mode"), "tile", None, None),
        P(("groups", "tile"), None),
        P(),
        P(),
        P(),
    )
    return jax.shard_map(
        body,
        mesh=mesh,
        in_specs=placed,
        out_specs=(
            P(None, ("groups", "energy", "mode"), "tile", None),
            P(None, None, ("groups", "energy", "mode"), None, None),
        ),
        check_vma=False,
    )
```

```python
import functools
import math

import jax
import jax.numpy as jnp
import ml_dtypes
import numpy as np
from jax import lax
from jax.experimental import pallas as pl
from jax.experimental.pallas import tpu as pltpu
from jax.sharding import PartitionSpec as P

PCOLS = 2
STEP = 32
LANES = 128
PAD_ROWS = 8


def swap_pairs(size, distance):
    return [(i, i ^ distance) for i in range(size)]


def dft_tables(extent):
    counter = np.arange(extent)
    phases = -2.0 * math.pi / extent * (counter[:, None] * counter[None, :] % extent)
    cosine = np.cos(phases) / math.sqrt(extent)
    sine = np.sin(phases) / math.sqrt(extent)
    forward = np.block([[cosine, -sine], [sine, cosine]])
    backward = np.block([[cosine, sine], [-sine, cosine]])
    return (
        jnp.asarray(forward.astype(np.float32).astype(ml_dtypes.bfloat16)),
        jnp.asarray(backward.astype(np.float32).astype(ml_dtypes.bfloat16)),
    )


def corner(offsets, q):
    row = STEP * (q // PCOLS) + offsets[0, q]
    col = STEP * (q % PCOLS) + offsets[1, q]
    return row, col


def spread(block, row):
    lane = lax.broadcasted_iota(jnp.int32, block.shape, 1)
    turned = pltpu.roll(block, row, 1)
    left = jnp.where(lane >= row, turned, 0.0)
    right = jnp.where(lane < row, turned, 0.0)
    return left, right


def round_kernel(offsets_hbm, object_hbm, message_ref, object_ref, offsets_ref, sems):
    cols, rows = object_ref.shape[1:]
    positions = offsets_ref.shape[1]
    copies = [pltpu.make_async_copy(offsets_hbm, offsets_ref, sems.at[2])]
    copies += [
        pltpu.make_async_copy(object_hbm.at[part, 0], object_ref.at[part], sems.at[part])
        for part in range(2)
    ]
    for copy in copies:
        copy.start()
    copies[0].wait()
    lane = lax.broadcasted_iota(jnp.int32, (PAD_ROWS, rows), 1)
    line = jnp.zeros((PAD_ROWS, rows), jnp.float32)
    for k in range(2):
        for q in range(positions):
            value = offsets_ref[k, q].astype(jnp.float32)
            line = jnp.where(lane == k * positions + q, value, line)
    message_ref[2 * cols :] = line.astype(jnp.bfloat16)
    for part in range(2):
        copies[1 + part].wait()
        message_ref[part * cols : (part + 1) * cols] = object_ref[part].astype(jnp.bfloat16)


def turn_kernel(
    offsets_hbm,
    analysis_hbm,
    basis_hbm,
    threshold_hbm,
    forward_hbm,
    backward_hbm,
    probe_hbm,
    moduli_hbm,
    offsets_out_ref,
    forward_ref,
    backward_ref,
    turned_ref,
    moduli_out_ref,
    power_ref,
    weight_ref,
    analysis_table_ref,
    last_table_ref,
    offsets_ref,
    analysis_ref,
    basis_ref,
    threshold_ref,
    probe_ref,
    moduli_ref,
    sems,
    *,
    sources,
    sizes,
):
    modes = probe_ref.shape[1]
    extent = probe_ref.shape[-1]
    positions = offsets_ref.shape[1]
    pairs = [
        (offsets_hbm, offsets_ref),
        (probe_hbm, probe_ref),
        (moduli_hbm, moduli_ref),
        (analysis_hbm, analysis_ref),
        (basis_hbm, basis_ref),
        (threshold_hbm, threshold_ref),
        (forward_hbm, forward_ref),
        (backward_hbm, backward_ref),
        (offsets_hbm, offsets_out_ref),
    ]
    copies = [
        pltpu.make_async_copy(source, target, sems.at[k])
        for k, (source, target) in enumerate(pairs)
    ]
    for copy in copies:
        copy.start()
    for copy in copies[3:6]:
        copy.wait()
    _, ms = sizes
    z = lax.axis_index("energy")
    m = lax.axis_index("mode")
    tile = analysis_table_ref.shape[2:]
    for k in range(threshold_ref.shape[0]):
        for number, (dz, dm) in enumerate(sources):
            label = (z ^ dz) * ms + (m ^ dm)
            analysis_table_ref[number, k] = jnp.full(tile, analysis_ref[k, label])
        last_table_ref[0, k] = jnp.full(tile, 0.5 * basis_ref[z * ms + m, k])
        last_table_ref[1, k] = jnp.full(tile, threshold_ref[k])
    copies[0].wait()
    copies[1].wait()
    power = jnp.zeros((extent, extent), jnp.float32)
    for part in range(2):
        for m in range(modes):
            value = probe_ref[part, m, 0].T
            turned_ref[part, m] = value
            power += value * value
    power_ref[...] = power
    weight_ref[...] = jnp.full_like(weight_ref, 0.1 * jnp.max(power) + 1e-06)
    for q in range(positions):
        row, col = corner(offsets_ref, q)
        left, _ = spread(power, row)
        weight_ref[pl.ds(col, extent)] += left
    copies[2].wait()
    for q in range(positions):
        moduli_out_ref[q] = moduli_ref[0, q].astype(jnp.float32).T
    for copy in copies[6:]:
        copy.wait()


def cut(extended, offsets_ref, q, extent):
    row, col = corner(offsets_ref, q)
    here = pl.ds(col, extent)
    lane = lax.broadcasted_iota(jnp.int32, (extent, extent), 1)
    found = []
    for part in range(2):
        left = pltpu.roll(extended[part, 0, here], extent - row, 1)
        right = pltpu.roll(extended[part, 1, here], extent - row, 1)
        found.append(jnp.where(lane < extent - row, left, right))
    return found


def extend(extended, own_ref, below_ref, tiles):
    cols = extended.shape[2]
    has_below = lax.axis_index("tile") < tiles - 1
    for part in range(2):
        here = slice(part * cols, (part + 1) * cols)
        extended[part, 0] = own_ref[here].astype(jnp.float32)
        extended[part, 1] = jnp.where(has_below, below_ref[here].astype(jnp.float32), 0.0)


def side_by_side(blocks):
    return jnp.concatenate(blocks, axis=1)


def stack_up(blocks):
    return jnp.concatenate(blocks, axis=0)


def wave_kernel(
    offsets_ref,
    own_ref,
    below_ref,
    probe_ref,
    moduli_ref,
    forward_ref,
    backward_ref,
    upper_ref,
    lower_ref,
    change_ref,
    window_ref,
    extended,
    total,
    *,
    tiles,
    group,
):
    extent = probe_ref.shape[-1]
    modes = probe_ref.shape[1]
    positions = offsets_ref.shape[1]
    waves = group * modes
    extend(extended, own_ref, below_ref, tiles)
    total[...] = jnp.zeros_like(total)
    low = slice(0, extent)
    high = slice(extent, 2 * extent)

    def dot(left, right):
        return jnp.dot(left, right, preferred_element_type=jnp.float32)

    def span(w):
        return slice(w * extent, (w + 1) * extent)

    def members(block):
        return [(member, block * group + member) for member in range(group)]

    def enter(block):
        rounded = []
        for member, q in members(block):
            object_real, object_imag = cut(extended, offsets_ref, q, extent)
            window_ref[q, 0] = object_real
            window_ref[q, 1] = object_imag
            for m in range(modes):
                probe_real = probe_ref[0, m]
                probe_imag = probe_ref[1, m]
                wave_real = probe_real * object_real - probe_imag * object_imag
                wave_imag = probe_real * object_imag + probe_imag * object_real
                change_ref[q, m, 0] = wave_real
                change_ref[q, m, 1] = wave_imag
                rounded.append(side_by_side([wave_real, wave_imag]).astype(jnp.bfloat16))
        return stack_up(rounded)

    def first_half(block, lying):
        halfway = dot(lying, backward_ref[...]).astype(jnp.bfloat16)
        return side_by_side(
            [stack_up([halfway[span(w), low], halfway[span(w), high]]) for w in range(waves)]
        )

    def project(block, standing):
        spectrum = dot(forward_ref[...], standing)
        scaled = []
        for member, q in members(block):
            magnitude = jnp.full((extent, extent), 0.01, jnp.float32)
            for m in range(modes):
                place = span(member * modes + m)
                real = spectrum[low, place]
                imag = spectrum[high, place]
                magnitude += real * real + imag * imag
            factor = moduli_ref[q] * lax.rsqrt(magnitude)
            for m in range(modes):
                place = span(member * modes + m)
                scaled.append(
                    stack_up([spectrum[low, place] * factor, spectrum[high, place] * factor]).astype(
                        jnp.bfloat16
                    )
                )
        return side_by_side(scaled)

    def second_half(block, standing):
        returned = dot(backward_ref[...], standing).astype(jnp.bfloat16)
        return stack_up(
            [side_by_side([returned[low, span(w)], returned[high, span(w)]]) for w in range(waves)]
        )

    def leave(block, lying):
        new_wave = dot(lying, forward_ref[...])
        for member, q in members(block):
            row, col = corner(offsets_ref, q)
            here = pl.ds(col, extent)
            sum_real = jnp.zeros((extent, extent), jnp.float32)
            sum_imag = jnp.zeros((extent, extent), jnp.float32)
            for m in range(modes):
                place = span(member * modes + m)
                change_real = new_wave[place, low] - change_ref[q, m, 0]
                change_imag = new_wave[place, high] - change_ref[q, m, 1]
                change_ref[q, m, 0] = change_real
                change_ref[q, m, 1] = change_imag
                probe_real = probe_ref[0, m]
                probe_imag = probe_ref[1, m]
                sum_real += probe_real * change_real + probe_imag * change_imag
                sum_imag += probe_real * change_imag - probe_imag * change_real
            for part, value in enumerate((sum_real, sum_imag)):
                for side, moved in enumerate(spread(value, row)):
                    total[part, side, here] += moved

    stages = [[enter], [first_half], [project], [second_half, leave]]
    blocks = positions // group
    held = [None] * blocks
    for tick in range(blocks + len(stages) - 1):
        for depth in range(len(stages)):
            block = tick - depth
            if not 0 <= block < blocks:
                continue
            for stage in stages[depth]:
                held[block] = stage(block) if stage is enter else stage(block, held[block])

    for part in range(2):
        upper_ref[part] = total[part, 0]
        lower_ref[part] = total[part, 1].astype(jnp.bfloat16)


def share_kernel(change_ref, window_ref, share_ref):
    extent = change_ref.shape[-1]
    positions, modes = change_ref.shape[:2]
    chunk = 32
    for start in range(0, extent, chunk):
        here = pl.ds(start, chunk)
        density = jnp.zeros((chunk, extent), jnp.float32)
        sums = [[jnp.zeros((chunk, extent), jnp.float32) for _ in range(2)] for _ in range(modes)]
        for q in range(positions):
            object_real = window_ref[q, 0, here]
            object_imag = window_ref[q, 1, here]
            density += object_real * object_real + object_imag * object_imag
            for m in range(modes):
                change_real = change_ref[q, m, 0, here]
                change_imag = change_ref[q, m, 1, here]
                sums[m][0] += object_real * change_real + object_imag * change_imag
                sums[m][1] += object_real * change_imag - object_imag * change_real
        for m in range(modes):
            for part in range(2):
                share_ref[part * modes + m, here] = sums[m][part].astype(jnp.bfloat16)
        share_ref[2 * modes, here] = density.astype(jnp.bfloat16)


def weight_kernel(above_ref, power_ref, weight_ref, inverse_ref, other, *, positions):
    extent = power_ref.shape[-1]
    cols = inverse_ref.shape[0]
    power = power_ref[...]
    other[...] = jnp.zeros_like(other)
    line = above_ref[2 * cols :].astype(jnp.float32)
    lane = lax.broadcasted_iota(jnp.int32, line.shape, 1)
    above = [
        jnp.max(jnp.where(lane == k, line, 0.0)).astype(jnp.int32) for k in range(2 * positions)
    ]
    for q in range(positions):
        row = STEP * (q // PCOLS) + above[q]
        col = STEP * (q % PCOLS) + above[positions + q]
        _, right = spread(power, row)
        other[pl.ds(col, extent)] += right
    has_above = lax.axis_index("tile") > 0
    inverse_ref[...] = 1.0 / (weight_ref[...] + jnp.where(has_above, other[...], 0.0))


def object_kernel(object_ref, upper_ref, received_ref, inverse_ref, new_ref, sent_ref):
    has_above = lax.axis_index("tile") > 0
    for part in range(2):
        received = received_ref[part].astype(jnp.float32)
        wave = upper_ref[part] + jnp.where(has_above, received, 0.0)
        value = object_ref[part] + wave * inverse_ref[...]
        new_ref[part] = value
        sent_ref[part] = value.astype(jnp.bfloat16)


def mix_kernel(table_ref, *refs, first, chained, chunk):
    mixed_ref = refs[-1]
    refs = refs[:-1]
    before, refs = (refs[0], refs[1:]) if chained else (None, refs)
    components, parts, rows, lanes = mixed_ref.shape
    height = table_ref.shape[2]
    folded = (chunk // height, height, lanes)
    for part in range(parts):
        for start in range(0, rows, chunk):
            here = pl.ds(start, chunk)
            values = [ref[part, here].astype(jnp.float32).reshape(folded) for ref in refs]
            for k in range(components):
                terms = [table_ref[first + n, k] * value for n, value in enumerate(values)]
                if before is not None:
                    terms.insert(0, before[k, part, here].reshape(folded))
                mixed_ref[k, part, here] = functools.reduce(jnp.add, terms).reshape(chunk, lanes)


def spectral_kernel(table_ref, last_ref, own_ref, mixed_ref, *refs, first, chunk):
    refs, (out_hbm, result, sems) = refs[:-3], refs[-3:]
    parts, rows, lanes = own_ref.shape
    components = last_ref.shape[1]
    height = table_ref.shape[2]
    folded = (chunk // height, height, lanes)
    copies = []
    for part in range(parts):
        for start in range(0, rows, chunk):
            here = pl.ds(start, chunk)
            values = [ref[part, here].astype(jnp.float32).reshape(folded) for ref in refs]
            terms = [0.5 * own_ref[part, here].reshape(folded)]
            for k in range(components):
                c = mixed_ref[k, part, here].reshape(folded)
                for n, value in enumerate(values):
                    c += table_ref[first + n, k] * value
                t = last_ref[1, k]
                c = c - jnp.minimum(jnp.maximum(c, -t), t)
                terms.append(last_ref[0, k] * c)
            while len(terms) > 1:
                terms = [sum(terms[k : k + 2][1:], terms[k]) for k in range(0, len(terms), 2)]
            result[part, here] = terms[0].reshape(chunk, lanes)
        copies.append(
            pltpu.make_async_copy(result.at[part], out_hbm.at[part, 0], sems.at[part])
        )
        copies[-1].start()
    for copy in copies:
        copy.wait()


def probe_kernel(probe_ref, own_ref, received_ref, out_ref):
    modes = probe_ref.shape[1]
    density = own_ref[2 * modes].astype(jnp.float32) + received_ref[2 * modes].astype(jnp.float32)
    inverse = 1.0 / (density + 0.1 * jnp.max(density) + 1e-06)
    for part in range(2):
        for m in range(modes):
            k = part * modes + m
            numerator = own_ref[k].astype(jnp.float32) + received_ref[k].astype(jnp.float32)
            out_ref[part, m, 0] = (probe_ref[part, m] + numerator * inverse).T


def call(kernel, inputs, places, outputs, scratch=(), limit=4, out="v"):
    kinds = {"s": pltpu.SMEM, "v": pltpu.VMEM, "h": pltpu.HBM}
    inputs = [
        pltpu.with_memory_space_constraint(x, pltpu.HBM) if p == "h" else x
        for x, p in zip(inputs, places)
    ]
    return pl.pallas_call(
        kernel,
        out_shape=outputs,
        in_specs=[pl.BlockSpec(memory_space=kinds[p]) for p in places],
        out_specs=jax.tree.map(lambda _: pl.BlockSpec(memory_space=kinds[out]), outputs),
        scratch_shapes=list(scratch),
        compiler_params=pltpu.CompilerParams(vmem_limit_bytes=limit << 20),
    )(*inputs)


def body(object_field, probe_field, modulus, offsets, spectra_basis, analysis, threshold):
    extent = probe_field.shape[-1]
    modes = probe_field.shape[1]
    object_field = jnp.transpose(object_field, (0, 1, 3, 2))
    offsets = jnp.transpose(offsets)
    cols, rows = object_field.shape[2:]
    positions = offsets.shape[1]
    tiles = lax.axis_size("tile")
    zs = lax.axis_size("energy")
    ms = lax.axis_size("mode")
    forward, backward = dft_tables(extent)
    shape = jax.ShapeDtypeStruct
    f32, bf16 = jnp.float32, jnp.bfloat16

    message, object_here = call(
        round_kernel,
        (offsets, object_field),
        "hh",
        (shape((2 * cols + PAD_ROWS, rows), bf16), shape((2, cols, rows), f32)),
        (pltpu.SMEM((2, positions), jnp.int32), pltpu.SemaphoreType.DMA((3,))),
    )
    if tiles == 2:
        below = above = lax.ppermute(message, "tile", swap_pairs(2, 1))
    else:
        below = lax.ppermute(message, "tile", [(i + 1, i) for i in range(tiles - 1)])
        above = lax.ppermute(message, "tile", [(i, i + 1) for i in range(tiles - 1)])

    near, far = gather_order(zs)[0], gather_order(zs)[-1]
    middle = [dz for dz in range(1, zs) if dz not in (near, far)]
    stages = [
        [(dz, dm) for dz in (0, near) for dm in range(ms)],
        [(dz, dm) for dz in middle for dm in range(ms)] + [(far, 0)],
        [(far, dm) for dm in range(1, ms)],
    ]
    sources = sum(stages, [])
    components = threshold.shape[0]
    offsets, forward, backward, turned, moduli, power, weight, table, last_table = call(
        functools.partial(turn_kernel, sources=tuple(sources), sizes=(zs, ms)),
        (offsets, analysis, spectra_basis, threshold, forward, backward, probe_field, modulus),
        "hhhhhhhh",
        (
            shape((2, positions), jnp.int32),
            shape(forward.shape, bf16),
            shape(backward.shape, bf16),
            shape((2, modes, extent, extent), f32),
            shape((positions, extent, extent), f32),
            shape((extent, extent), f32),
            shape((cols, rows), f32),
            shape((len(sources), components, 8, LANES), f32),
            shape((2, components, 8, LANES), f32),
        ),
        (
            pltpu.SMEM((2, positions), jnp.int32),
            pltpu.SMEM(analysis.shape, f32),
            pltpu.SMEM(spectra_basis.shape, f32),
            pltpu.SMEM(threshold.shape, f32),
            pltpu.VMEM(probe_field.shape, f32),
            pltpu.VMEM(modulus.shape, bf16),
            pltpu.SemaphoreType.DMA((9,)),
        ),
        limit=8,
    )
    upper, lower, change, window = call(
        functools.partial(wave_kernel, tiles=tiles, group=2),
        (offsets, message, below, turned, moduli, forward, backward),
        "svvvvvv",
        (
            shape((2, cols, rows), f32),
            shape((2, cols, rows), bf16),
            shape((positions, modes, 2, extent, extent), f32),
            shape((positions, 2, extent, extent), f32),
        ),
        (
            pltpu.VMEM((2, 2, cols, LANES), f32),
            pltpu.VMEM((2, 2, cols, LANES), f32),
        ),
        limit=24,
    )
    if tiles == 2:
        received = lax.ppermute(lower, "tile", swap_pairs(2, 1))
    else:
        received = lax.ppermute(lower, "tile", [(i, i + 1) for i in range(tiles - 1)])
    inverse = call(
        functools.partial(weight_kernel, positions=positions),
        (above, power, weight),
        "vvv",
        shape((cols, rows), f32),
        (pltpu.VMEM((cols, rows), f32),),
    )
    share = call(share_kernel, (change, window), "vv", shape((2 * modes + 1, extent, extent), bf16))
    object_new, sent = call(
        object_kernel,
        (object_here, upper, received, inverse),
        "vvvv",
        (shape((2, cols, rows), f32), shape((2, cols, rows), bf16)),
    )
    pieces = {(0, 0): sent}
    for dz in range(1, zs):
        pieces[dz, 0] = lax.ppermute(sent, "energy", swap_pairs(zs, dz))
    for dz in range(zs):
        for dm in range(1, ms):
            pieces[dz, dm] = lax.ppermute(pieces[dz, 0], "mode", swap_pairs(ms, dm))
    mixed = None
    first = 0
    for stage in stages[:2]:
        inputs = [table] + ([] if mixed is None else [mixed]) + [pieces[s] for s in stage]
        mixed = call(
            functools.partial(mix_kernel, first=first, chained=mixed is not None, chunk=64),
            inputs,
            "v" * len(inputs),
            shape((components, 2, cols, rows), f32),
        )
        first += len(stage)
    inputs = [table, last_table, object_new, mixed] + [pieces[s] for s in stages[2]]
    object_out = call(
        functools.partial(spectral_kernel, first=first, chunk=64),
        inputs,
        "v" * len(inputs),
        shape(object_field.shape, f32),
        (pltpu.VMEM((2, cols, rows), f32), pltpu.SemaphoreType.DMA((2,))),
        out="h",
    )
    for distance in [1 << k for k in range(1, tiles.bit_length() - 1)]:
        other = lax.ppermute(share, "tile", swap_pairs(tiles, distance))
        share = (share.astype(f32) + other.astype(f32)).astype(bf16)
    other = lax.ppermute(share, "tile", swap_pairs(tiles, 1))
    probe_out = call(probe_kernel, (turned, share, other), "vvv", shape(probe_field.shape, f32))
    return (jnp.transpose(object_out, (0, 1, 3, 2)), probe_out)


def gather_order(zs):
    return [zs // 2] + [dz for dz in range(1, zs) if dz != zs // 2]


def solution(mesh):
    placed = (
        P(None, ("groups", "energy", "mode"), "tile", None),
        P(None, None, ("groups", "energy", "mode"), None, None),
        P(("groups", "energy", "mode"), "tile", None, None),
        P(("groups", "tile"), None),
        P(),
        P(),
        P(),
    )
    return jax.shard_map(
        body,
        mesh=mesh,
        in_specs=placed,
        out_specs=(
            P(None, ("groups", "energy", "mode"), "tile", None),
            P(None, None, ("groups", "energy", "mode"), None, None),
        ),
        check_vma=False,
    )
```

```python
import functools
import math

import jax
import jax.numpy as jnp
import ml_dtypes
import numpy as np
from jax import lax
from jax.experimental import pallas as pl
from jax.experimental.pallas import tpu as pltpu
from jax.sharding import PartitionSpec as P

PCOLS = 2
STEP = 32
LANES = 128
PAD_ROWS = 8


def swap_pairs(size, distance):
    return [(i, i ^ distance) for i in range(size)]


def dft_tables(extent):
    counter = np.arange(extent)
    phases = -2.0 * math.pi / extent * (counter[:, None] * counter[None, :] % extent)
    cosine = np.cos(phases) / math.sqrt(extent)
    sine = np.sin(phases) / math.sqrt(extent)
    forward = np.block([[cosine, -sine], [sine, cosine]])
    backward = np.block([[cosine, sine], [-sine, cosine]])
    return (
        jnp.asarray(forward.astype(np.float32).astype(ml_dtypes.bfloat16)),
        jnp.asarray(backward.astype(np.float32).astype(ml_dtypes.bfloat16)),
    )


def corner(offsets, q):
    row = STEP * (q // PCOLS) + offsets[0, q]
    col = STEP * (q % PCOLS) + offsets[1, q]
    return row, col


def spread(block, row):
    lane = lax.broadcasted_iota(jnp.int32, block.shape, 1)
    turned = pltpu.roll(block, row, 1)
    left = jnp.where(lane >= row, turned, 0.0)
    right = jnp.where(lane < row, turned, 0.0)
    return left, right


def round_kernel(offsets_hbm, object_hbm, message_ref, object_ref, offsets_ref, sems):
    cols, rows = object_ref.shape[1:]
    positions = offsets_ref.shape[1]
    copies = [pltpu.make_async_copy(offsets_hbm, offsets_ref, sems.at[2])]
    copies += [
        pltpu.make_async_copy(object_hbm.at[part, 0], object_ref.at[part], sems.at[part])
        for part in range(2)
    ]
    for copy in copies:
        copy.start()
    copies[0].wait()
    lane = lax.broadcasted_iota(jnp.int32, (PAD_ROWS, rows), 1)
    line = jnp.zeros((PAD_ROWS, rows), jnp.float32)
    for k in range(2):
        for q in range(positions):
            value = offsets_ref[k, q].astype(jnp.float32)
            line = jnp.where(lane == k * positions + q, value, line)
    message_ref[2 * cols :] = line.astype(jnp.bfloat16)
    for part in range(2):
        copies[1 + part].wait()
        message_ref[part * cols : (part + 1) * cols] = object_ref[part].astype(jnp.bfloat16)


def turn_kernel(
    offsets_hbm,
    analysis_hbm,
    basis_hbm,
    threshold_hbm,
    forward_hbm,
    backward_hbm,
    probe_hbm,
    moduli_hbm,
    offsets_out_ref,
    forward_ref,
    backward_ref,
    turned_ref,
    moduli_out_ref,
    power_ref,
    weight_ref,
    analysis_table_ref,
    last_table_ref,
    offsets_ref,
    analysis_ref,
    basis_ref,
    threshold_ref,
    probe_ref,
    moduli_ref,
    sems,
    *,
    sources,
    sizes,
):
    modes = probe_ref.shape[1]
    extent = probe_ref.shape[-1]
    positions = offsets_ref.shape[1]
    pairs = [
        (offsets_hbm, offsets_ref),
        (probe_hbm, probe_ref),
        (moduli_hbm, moduli_ref),
        (analysis_hbm, analysis_ref),
        (basis_hbm, basis_ref),
        (threshold_hbm, threshold_ref),
        (forward_hbm, forward_ref),
        (backward_hbm, backward_ref),
        (offsets_hbm, offsets_out_ref),
    ]
    copies = [
        pltpu.make_async_copy(source, target, sems.at[k])
        for k, (source, target) in enumerate(pairs)
    ]
    for copy in copies:
        copy.start()
    for copy in copies[3:6]:
        copy.wait()
    _, ms = sizes
    z = lax.axis_index("energy")
    m = lax.axis_index("mode")
    tile = analysis_table_ref.shape[2:]
    for k in range(threshold_ref.shape[0]):
        for number, (dz, dm) in enumerate(sources):
            label = (z ^ dz) * ms + (m ^ dm)
            analysis_table_ref[number, k] = jnp.full(tile, analysis_ref[k, label])
        last_table_ref[0, k] = jnp.full(tile, 0.5 * basis_ref[z * ms + m, k])
        last_table_ref[1, k] = jnp.full(tile, threshold_ref[k])
    copies[0].wait()
    copies[1].wait()
    power = jnp.zeros((extent, extent), jnp.float32)
    for part in range(2):
        for m in range(modes):
            value = probe_ref[part, m, 0].T
            turned_ref[part, m] = value
            power += value * value
    power_ref[...] = power
    weight_ref[...] = jnp.full_like(weight_ref, 0.1 * jnp.max(power) + 1e-06)
    for q in range(positions):
        row, col = corner(offsets_ref, q)
        left, _ = spread(power, row)
        weight_ref[pl.ds(col, extent)] += left
    copies[2].wait()
    for q in range(positions):
        moduli_out_ref[q] = moduli_ref[0, q].astype(jnp.float32).T
    for copy in copies[6:]:
        copy.wait()


def cut(extended, offsets_ref, q, extent):
    row, col = corner(offsets_ref, q)
    here = pl.ds(col, extent)
    lane = lax.broadcasted_iota(jnp.int32, (extent, extent), 1)
    found = []
    for part in range(2):
        left = pltpu.roll(extended[part, 0, here], extent - row, 1)
        right = pltpu.roll(extended[part, 1, here], extent - row, 1)
        found.append(jnp.where(lane < extent - row, left, right))
    return found


def extend(extended, own_ref, below_ref, tiles):
    cols = extended.shape[2]
    has_below = lax.axis_index("tile") < tiles - 1
    for part in range(2):
        here = slice(part * cols, (part + 1) * cols)
        extended[part, 0] = own_ref[here].astype(jnp.float32)
        extended[part, 1] = jnp.where(has_below, below_ref[here].astype(jnp.float32), 0.0)


def side_by_side(blocks):
    return jnp.concatenate(blocks, axis=1)


def stack_up(blocks):
    return jnp.concatenate(blocks, axis=0)


def wave_kernel(
    offsets_ref,
    own_ref,
    below_ref,
    probe_ref,
    moduli_ref,
    forward_ref,
    backward_ref,
    upper_ref,
    lower_ref,
    change_ref,
    window_ref,
    extended,
    total,
    *,
    tiles,
    group,
):
    extent = probe_ref.shape[-1]
    modes = probe_ref.shape[1]
    positions = offsets_ref.shape[1]
    waves = group * modes
    extend(extended, own_ref, below_ref, tiles)
    total[...] = jnp.zeros_like(total)
    low = slice(0, extent)
    high = slice(extent, 2 * extent)

    def dot(left, right):
        return jnp.dot(left, right, preferred_element_type=jnp.float32)

    def span(w):
        return slice(w * extent, (w + 1) * extent)

    def members(block):
        return [(member, block * group + member) for member in range(group)]

    def enter(block):
        rounded = []
        for member, q in members(block):
            object_real, object_imag = cut(extended, offsets_ref, q, extent)
            window_ref[q, 0] = object_real
            window_ref[q, 1] = object_imag
            for m in range(modes):
                probe_real = probe_ref[0, m]
                probe_imag = probe_ref[1, m]
                wave_real = probe_real * object_real - probe_imag * object_imag
                wave_imag = probe_real * object_imag + probe_imag * object_real
                change_ref[q, m, 0] = wave_real
                change_ref[q, m, 1] = wave_imag
                rounded.append(side_by_side([wave_real, wave_imag]).astype(jnp.bfloat16))
        return stack_up(rounded)

    def first_half(block, lying):
        halfway = dot(lying, backward_ref[...]).astype(jnp.bfloat16)
        return side_by_side(
            [stack_up([halfway[span(w), low], halfway[span(w), high]]) for w in range(waves)]
        )

    def project(block, standing):
        spectrum = dot(forward_ref[...], standing)
        scaled = []
        for member, q in members(block):
            magnitude = jnp.full((extent, extent), 0.01, jnp.float32)
            for m in range(modes):
                place = span(member * modes + m)
                real = spectrum[low, place]
                imag = spectrum[high, place]
                magnitude += real * real + imag * imag
            factor = moduli_ref[q] * lax.rsqrt(magnitude)
            for m in range(modes):
                place = span(member * modes + m)
                scaled.append(
                    stack_up([spectrum[low, place] * factor, spectrum[high, place] * factor]).astype(
                        jnp.bfloat16
                    )
                )
        return side_by_side(scaled)

    def second_half(block, standing):
        returned = dot(backward_ref[...], standing).astype(jnp.bfloat16)
        return stack_up(
            [side_by_side([returned[low, span(w)], returned[high, span(w)]]) for w in range(waves)]
        )

    def leave(block, lying):
        new_wave = dot(lying, forward_ref[...])
        for member, q in members(block):
            row, col = corner(offsets_ref, q)
            here = pl.ds(col, extent)
            sum_real = jnp.zeros((extent, extent), jnp.float32)
            sum_imag = jnp.zeros((extent, extent), jnp.float32)
            for m in range(modes):
                place = span(member * modes + m)
                change_real = new_wave[place, low] - change_ref[q, m, 0]
                change_imag = new_wave[place, high] - change_ref[q, m, 1]
                change_ref[q, m, 0] = change_real
                change_ref[q, m, 1] = change_imag
                probe_real = probe_ref[0, m]
                probe_imag = probe_ref[1, m]
                sum_real += probe_real * change_real + probe_imag * change_imag
                sum_imag += probe_real * change_imag - probe_imag * change_real
            for part, value in enumerate((sum_real, sum_imag)):
                for side, moved in enumerate(spread(value, row)):
                    total[part, side, here] += moved

    stages = [[enter], [first_half], [project], [second_half, leave]]
    blocks = positions // group
    held = [None] * blocks
    for tick in range(blocks + len(stages) - 1):
        for depth in range(len(stages)):
            block = tick - depth
            if not 0 <= block < blocks:
                continue
            for stage in stages[depth]:
                held[block] = stage(block) if stage is enter else stage(block, held[block])

    for part in range(2):
        upper_ref[part] = total[part, 0]
        lower_ref[part] = total[part, 1].astype(jnp.bfloat16)


def share_kernel(change_ref, window_ref, share_ref):
    extent = change_ref.shape[-1]
    positions, modes = change_ref.shape[:2]
    chunk = 32
    for start in range(0, extent, chunk):
        here = pl.ds(start, chunk)
        density = jnp.zeros((chunk, extent), jnp.float32)
        sums = [[jnp.zeros((chunk, extent), jnp.float32) for _ in range(2)] for _ in range(modes)]
        for q in range(positions):
            object_real = window_ref[q, 0, here]
            object_imag = window_ref[q, 1, here]
            density += object_real * object_real + object_imag * object_imag
            for m in range(modes):
                change_real = change_ref[q, m, 0, here]
                change_imag = change_ref[q, m, 1, here]
                sums[m][0] += object_real * change_real + object_imag * change_imag
                sums[m][1] += object_real * change_imag - object_imag * change_real
        for m in range(modes):
            for part in range(2):
                share_ref[part * modes + m, here] = sums[m][part].astype(jnp.bfloat16)
        share_ref[2 * modes, here] = density.astype(jnp.bfloat16)


def weight_kernel(above_ref, power_ref, weight_ref, inverse_ref, other, *, positions):
    extent = power_ref.shape[-1]
    cols = inverse_ref.shape[0]
    power = power_ref[...]
    other[...] = jnp.zeros_like(other)
    line = above_ref[2 * cols :].astype(jnp.float32)
    lane = lax.broadcasted_iota(jnp.int32, line.shape, 1)
    above = [
        jnp.max(jnp.where(lane == k, line, 0.0)).astype(jnp.int32) for k in range(2 * positions)
    ]
    for q in range(positions):
        row = STEP * (q // PCOLS) + above[q]
        col = STEP * (q % PCOLS) + above[positions + q]
        _, right = spread(power, row)
        other[pl.ds(col, extent)] += right
    has_above = lax.axis_index("tile") > 0
    inverse_ref[...] = 1.0 / (weight_ref[...] + jnp.where(has_above, other[...], 0.0))


def object_kernel(object_ref, upper_ref, received_ref, inverse_ref, new_ref, sent_ref):
    has_above = lax.axis_index("tile") > 0
    for part in range(2):
        received = received_ref[part].astype(jnp.float32)
        wave = upper_ref[part] + jnp.where(has_above, received, 0.0)
        value = object_ref[part] + wave * inverse_ref[...]
        new_ref[part] = value
        sent_ref[part] = value.astype(jnp.bfloat16)


def mix_kernel(table_ref, *refs, first, chained, chunk):
    mixed_ref = refs[-1]
    refs = refs[:-1]
    before, refs = (refs[0], refs[1:]) if chained else (None, refs)
    components, parts, rows, lanes = mixed_ref.shape
    height = table_ref.shape[2]
    folded = (chunk // height, height, lanes)
    for part in range(parts):
        for start in range(0, rows, chunk):
            here = pl.ds(start, chunk)
            values = [ref[part, here].astype(jnp.float32).reshape(folded) for ref in refs]
            for k in range(components):
                terms = [table_ref[first + n, k] * value for n, value in enumerate(values)]
                if before is not None:
                    terms.insert(0, before[k, part, here].reshape(folded))
                mixed_ref[k, part, here] = functools.reduce(jnp.add, terms).reshape(chunk, lanes)


def finish_kernel(probe_ref, table_ref, last_ref, own_ref, mixed_ref, *refs, first, chunk):
    refs, (out_hbm, probe_hbm, result, sems) = refs[:-4], refs[-4:]
    parts, rows, lanes = own_ref.shape
    components = last_ref.shape[1]
    height = table_ref.shape[2]
    folded = (chunk // height, height, lanes)
    copies = [pltpu.make_async_copy(probe_ref, probe_hbm, sems.at[0])]
    copies[0].start()
    for part in range(parts):
        for start in range(0, rows, chunk):
            here = pl.ds(start, chunk)
            values = [ref[part, here].astype(jnp.float32).reshape(folded) for ref in refs]
            terms = [0.5 * own_ref[part, here].reshape(folded)]
            for k in range(components):
                c = mixed_ref[k, part, here].reshape(folded)
                for n, value in enumerate(values):
                    c += table_ref[first + n, k] * value
                t = last_ref[1, k]
                c = c - jnp.minimum(jnp.maximum(c, -t), t)
                terms.append(last_ref[0, k] * c)
            while len(terms) > 1:
                terms = [sum(terms[k : k + 2][1:], terms[k]) for k in range(0, len(terms), 2)]
            result[part, here] = terms[0].reshape(chunk, lanes)
            source, target = result.at[part, here], out_hbm.at[part, 0, here]
            copies.append(pltpu.make_async_copy(source, target, sems.at[len(copies)]))
            copies[-1].start()
    for copy in copies:
        copy.wait()


def probe_kernel(probe_ref, own_ref, received_ref, new_ref):
    modes = probe_ref.shape[1]
    density = own_ref[2 * modes].astype(jnp.float32) + received_ref[2 * modes].astype(jnp.float32)
    inverse = 1.0 / (density + 0.1 * jnp.max(density) + 1e-06)
    for part in range(2):
        for m in range(modes):
            k = part * modes + m
            numerator = own_ref[k].astype(jnp.float32) + received_ref[k].astype(jnp.float32)
            new_ref[part, m, 0] = (probe_ref[part, m] + numerator * inverse).T


def call(kernel, inputs, places, outputs, scratch=(), limit=4, out="v"):
    kinds = {"s": pltpu.SMEM, "v": pltpu.VMEM, "h": pltpu.HBM}
    inputs = [
        pltpu.with_memory_space_constraint(x, pltpu.HBM) if p == "h" else x
        for x, p in zip(inputs, places)
    ]
    return pl.pallas_call(
        kernel,
        out_shape=outputs,
        in_specs=[pl.BlockSpec(memory_space=kinds[p]) for p in places],
        out_specs=jax.tree.map(lambda _: pl.BlockSpec(memory_space=kinds[out]), outputs),
        scratch_shapes=list(scratch),
        compiler_params=pltpu.CompilerParams(vmem_limit_bytes=limit << 20),
    )(*inputs)


def body(object_field, probe_field, modulus, offsets, spectra_basis, analysis, threshold):
    extent = probe_field.shape[-1]
    modes = probe_field.shape[1]
    object_field = jnp.transpose(object_field, (0, 1, 3, 2))
    offsets = jnp.transpose(offsets)
    cols, rows = object_field.shape[2:]
    positions = offsets.shape[1]
    tiles = lax.axis_size("tile")
    zs = lax.axis_size("energy")
    ms = lax.axis_size("mode")
    forward, backward = dft_tables(extent)
    shape = jax.ShapeDtypeStruct
    f32, bf16 = jnp.float32, jnp.bfloat16

    message, object_here = call(
        round_kernel,
        (offsets, object_field),
        "hh",
        (shape((2 * cols + PAD_ROWS, rows), bf16), shape((2, cols, rows), f32)),
        (pltpu.SMEM((2, positions), jnp.int32), pltpu.SemaphoreType.DMA((3,))),
    )
    if tiles == 2:
        below = above = lax.ppermute(message, "tile", swap_pairs(2, 1))
    else:
        below = lax.ppermute(message, "tile", [(i + 1, i) for i in range(tiles - 1)])
        above = lax.ppermute(message, "tile", [(i, i + 1) for i in range(tiles - 1)])

    near, far = zs - 1, zs // 2
    middle = [dz for dz in range(1, zs) if dz not in (near, far)]
    stages = [
        [(dz, dm) for dz in (0, near) for dm in range(ms)],
        [(dz, dm) for dz in middle for dm in range(ms)] + [(far, 0)],
        [(far, dm) for dm in range(1, ms)],
    ]
    sources = sum(stages, [])
    components = threshold.shape[0]
    offsets, forward, backward, turned, moduli, power, weight, table, last_table = call(
        functools.partial(turn_kernel, sources=tuple(sources), sizes=(zs, ms)),
        (offsets, analysis, spectra_basis, threshold, forward, backward, probe_field, modulus),
        "hhhhhhhh",
        (
            shape((2, positions), jnp.int32),
            shape(forward.shape, bf16),
            shape(backward.shape, bf16),
            shape((2, modes, extent, extent), f32),
            shape((positions, extent, extent), f32),
            shape((extent, extent), f32),
            shape((cols, rows), f32),
            shape((len(sources), components, 8, LANES), f32),
            shape((2, components, 8, LANES), f32),
        ),
        (
            pltpu.SMEM((2, positions), jnp.int32),
            pltpu.SMEM(analysis.shape, f32),
            pltpu.SMEM(spectra_basis.shape, f32),
            pltpu.SMEM(threshold.shape, f32),
            pltpu.VMEM(probe_field.shape, f32),
            pltpu.VMEM(modulus.shape, bf16),
            pltpu.SemaphoreType.DMA((9,)),
        ),
        limit=8,
    )
    upper, lower, change, window = call(
        functools.partial(wave_kernel, tiles=tiles, group=2),
        (offsets, message, below, turned, moduli, forward, backward),
        "svvvvvv",
        (
            shape((2, cols, rows), f32),
            shape((2, cols, rows), bf16),
            shape((positions, modes, 2, extent, extent), f32),
            shape((positions, 2, extent, extent), f32),
        ),
        (
            pltpu.VMEM((2, 2, cols, LANES), f32),
            pltpu.VMEM((2, 2, cols, LANES), f32),
        ),
        limit=24,
    )
    if tiles == 2:
        received = lax.ppermute(lower, "tile", swap_pairs(2, 1))
    else:
        received = lax.ppermute(lower, "tile", [(i, i + 1) for i in range(tiles - 1)])
    inverse = call(
        functools.partial(weight_kernel, positions=positions),
        (above, power, weight),
        "vvv",
        shape((cols, rows), f32),
        (pltpu.VMEM((cols, rows), f32),),
    )
    share = call(share_kernel, (change, window), "vv", shape((2 * modes + 1, extent, extent), bf16))
    object_new, sent = call(
        object_kernel,
        (object_here, upper, received, inverse),
        "vvvv",
        (shape((2, cols, rows), f32), shape((2, cols, rows), bf16)),
    )
    pieces = {(0, 0): sent}
    for dz in range(1, zs):
        pieces[dz, 0] = lax.ppermute(sent, "energy", swap_pairs(zs, dz))
    for dz in range(zs):
        for dm in range(1, ms):
            pieces[dz, dm] = lax.ppermute(pieces[dz, 0], "mode", swap_pairs(ms, dm))
    mixed = None
    first = 0
    for stage in stages[:2]:
        inputs = [table] + ([] if mixed is None else [mixed]) + [pieces[s] for s in stage]
        mixed = call(
            functools.partial(mix_kernel, first=first, chained=mixed is not None, chunk=64),
            inputs,
            "v" * len(inputs),
            shape((components, 2, cols, rows), f32),
        )
        first += len(stage)
    for distance in [1 << k for k in range(1, tiles.bit_length() - 1)]:
        other = lax.ppermute(share, "tile", swap_pairs(tiles, distance))
        share = (share.astype(f32) + other.astype(f32)).astype(bf16)
    other = lax.ppermute(share, "tile", swap_pairs(tiles, 1))
    probe_new = call(probe_kernel, (turned, share, other), "vvv", shape(probe_field.shape, f32))
    inputs = [probe_new, table, last_table, object_new, mixed] + [pieces[s] for s in stages[2]]
    object_out, probe_out = call(
        functools.partial(finish_kernel, first=first, chunk=64),
        inputs,
        "v" * len(inputs),
        (shape(object_field.shape, f32), shape(probe_field.shape, f32)),
        (pltpu.VMEM((2, cols, rows), f32), pltpu.SemaphoreType.DMA((1 + 2 * cols // 64,))),
        out="h",
    )
    return (jnp.transpose(object_out, (0, 1, 3, 2)), probe_out)


def solution(mesh):
    placed = (
        P(None, ("groups", "energy", "mode"), "tile", None),
        P(None, None, ("groups", "energy", "mode"), None, None),
        P(("groups", "energy", "mode"), "tile", None, None),
        P(("groups", "tile"), None),
        P(),
        P(),
        P(),
    )
    return jax.shard_map(
        body,
        mesh=mesh,
        in_specs=placed,
        out_specs=(
            P(None, ("groups", "energy", "mode"), "tile", None),
            P(None, None, ("groups", "energy", "mode"), None, None),
        ),
        check_vma=False,
    )
```

```python
import functools
import math

import jax
import jax.numpy as jnp
import ml_dtypes
import numpy as np
from jax import lax
from jax.experimental import pallas as pl
from jax.experimental.pallas import tpu as pltpu
from jax.sharding import PartitionSpec as P

PCOLS = 2
STEP = 32
LANES = 128
PAD_ROWS = 8


def swap_pairs(size, distance):
    return [(i, i ^ distance) for i in range(size)]


def dft_tables(extent):
    counter = np.arange(extent)
    phases = -2.0 * math.pi / extent * (counter[:, None] * counter[None, :] % extent)
    cosine = np.cos(phases) / math.sqrt(extent)
    sine = np.sin(phases) / math.sqrt(extent)
    forward = np.block([[cosine, -sine], [sine, cosine]])
    backward = np.block([[cosine, sine], [-sine, cosine]])
    return (
        jnp.asarray(forward.astype(np.float32).astype(ml_dtypes.bfloat16)),
        jnp.asarray(backward.astype(np.float32).astype(ml_dtypes.bfloat16)),
    )


def corner(offsets, q):
    row = STEP * (q // PCOLS) + offsets[0, q]
    col = STEP * (q % PCOLS) + offsets[1, q]
    return row, col


def spread(block, row):
    lane = lax.broadcasted_iota(jnp.int32, block.shape, 1)
    turned = pltpu.roll(block, row, 1)
    left = jnp.where(lane >= row, turned, 0.0)
    right = jnp.where(lane < row, turned, 0.0)
    return left, right


def round_kernel(offsets_hbm, object_hbm, message_ref, object_ref, offsets_ref, sems):
    cols, rows = object_ref.shape[1:]
    positions = offsets_ref.shape[1]
    copies = [pltpu.make_async_copy(offsets_hbm, offsets_ref, sems.at[2])]
    copies += [
        pltpu.make_async_copy(object_hbm.at[part, 0], object_ref.at[part], sems.at[part])
        for part in range(2)
    ]
    for copy in copies:
        copy.start()
    copies[0].wait()
    lane = lax.broadcasted_iota(jnp.int32, (PAD_ROWS, rows), 1)
    line = jnp.zeros((PAD_ROWS, rows), jnp.float32)
    for k in range(2):
        for q in range(positions):
            value = offsets_ref[k, q].astype(jnp.float32)
            line = jnp.where(lane == k * positions + q, value, line)
    message_ref[2 * cols :] = line.astype(jnp.bfloat16)
    for part in range(2):
        copies[1 + part].wait()
        message_ref[part * cols : (part + 1) * cols] = object_ref[part].astype(jnp.bfloat16)


def turn_kernel(
    offsets_hbm,
    analysis_hbm,
    basis_hbm,
    threshold_hbm,
    forward_hbm,
    backward_hbm,
    probe_hbm,
    moduli_hbm,
    offsets_out_ref,
    forward_ref,
    backward_ref,
    turned_ref,
    moduli_out_ref,
    power_ref,
    weight_ref,
    analysis_table_ref,
    last_table_ref,
    late_table_ref,
    offsets_ref,
    analysis_ref,
    basis_ref,
    threshold_ref,
    probe_ref,
    moduli_ref,
    sems,
    *,
    sources,
    sizes,
):
    modes = probe_ref.shape[1]
    extent = probe_ref.shape[-1]
    positions = offsets_ref.shape[1]
    pairs = [
        (offsets_hbm, offsets_ref),
        (probe_hbm, probe_ref),
        (moduli_hbm, moduli_ref),
        (analysis_hbm, analysis_ref),
        (basis_hbm, basis_ref),
        (threshold_hbm, threshold_ref),
        (forward_hbm, forward_ref),
        (backward_hbm, backward_ref),
        (offsets_hbm, offsets_out_ref),
    ]
    copies = [
        pltpu.make_async_copy(source, target, sems.at[k])
        for k, (source, target) in enumerate(pairs)
    ]
    for copy in copies:
        copy.start()
    for copy in copies[3:6]:
        copy.wait()
    _, ms = sizes
    z = lax.axis_index("energy")
    m = lax.axis_index("mode")
    tile = analysis_table_ref.shape[2:]
    late = [0.0] * len(sources)
    for k in range(threshold_ref.shape[0]):
        half = 0.5 * basis_ref[z * ms + m, k]
        for number, (dz, dm) in enumerate(sources):
            label = (z ^ dz) * ms + (m ^ dm)
            weight = half * analysis_ref[k, label]
            analysis_table_ref[number, k] = jnp.full(tile, weight)
            late[number] += weight
        last_table_ref[k] = jnp.full(tile, jnp.maximum(half, -half) * threshold_ref[k])
    for number in range(len(sources)):
        late_table_ref[number] = jnp.full(tile, late[number])
    copies[0].wait()
    copies[1].wait()
    power = jnp.zeros((extent, extent), jnp.float32)
    for part in range(2):
        for m in range(modes):
            value = probe_ref[part, m, 0].T
            turned_ref[part, m] = value
            power += value * value
    power_ref[...] = power
    weight_ref[...] = jnp.full_like(weight_ref, 0.1 * jnp.max(power) + 1e-06)
    for q in range(positions):
        row, col = corner(offsets_ref, q)
        left, _ = spread(power, row)
        weight_ref[pl.ds(col, extent)] += left
    copies[2].wait()
    for q in range(positions):
        moduli_out_ref[q] = moduli_ref[0, q].astype(jnp.float32).T
    for copy in copies[6:]:
        copy.wait()


def cut(extended, offsets_ref, q, extent):
    row, col = corner(offsets_ref, q)
    here = pl.ds(col, extent)
    lane = lax.broadcasted_iota(jnp.int32, (extent, extent), 1)
    found = []
    amount = lax.rem(extent - row, extent)
    for part in range(2):
        left = pltpu.roll(extended[part, 0, here], amount, 1)
        right = pltpu.roll(extended[part, 1, here], amount, 1)
        found.append(jnp.where(lane < extent - row, left, right))
    return found


def extend(extended, own_ref, below_ref, tiles):
    cols = extended.shape[2]
    has_below = lax.axis_index("tile") < tiles - 1
    for part in range(2):
        here = slice(part * cols, (part + 1) * cols)
        extended[part, 0] = own_ref[here].astype(jnp.float32)
        extended[part, 1] = jnp.where(has_below, below_ref[here].astype(jnp.float32), 0.0)


def side_by_side(blocks):
    return jnp.concatenate(blocks, axis=1)


def stack_up(blocks):
    return jnp.concatenate(blocks, axis=0)


def wave_kernel(
    offsets_ref,
    own_ref,
    below_ref,
    probe_ref,
    moduli_ref,
    forward_ref,
    backward_ref,
    upper_ref,
    lower_ref,
    change_ref,
    window_ref,
    extended,
    total,
    *,
    tiles,
    group,
):
    extent = probe_ref.shape[-1]
    modes = probe_ref.shape[1]
    positions = offsets_ref.shape[1]
    waves = group * modes
    extend(extended, own_ref, below_ref, tiles)
    total[...] = jnp.zeros_like(total)
    low = slice(0, extent)
    high = slice(extent, 2 * extent)

    def dot(left, right):
        return jnp.dot(left, right, preferred_element_type=jnp.float32)

    def span(w):
        return slice(w * extent, (w + 1) * extent)

    def members(block):
        return [(member, block * group + member) for member in range(group)]

    def enter(block):
        rounded = []
        for member, q in members(block):
            object_real, object_imag = cut(extended, offsets_ref, q, extent)
            window_ref[q, 0] = object_real
            window_ref[q, 1] = object_imag
            for m in range(modes):
                probe_real = probe_ref[0, m]
                probe_imag = probe_ref[1, m]
                wave_real = probe_real * object_real - probe_imag * object_imag
                wave_imag = probe_real * object_imag + probe_imag * object_real
                change_ref[q, m, 0] = wave_real
                change_ref[q, m, 1] = wave_imag
                rounded.append(side_by_side([wave_real, wave_imag]).astype(jnp.bfloat16))
        return stack_up(rounded)

    def first_half(block, lying):
        halfway = dot(lying, backward_ref[...]).astype(jnp.bfloat16)
        return side_by_side(
            [stack_up([halfway[span(w), low], halfway[span(w), high]]) for w in range(waves)]
        )

    def project(block, standing):
        spectrum = dot(forward_ref[...], standing)
        scaled = []
        for member, q in members(block):
            magnitude = jnp.full((extent, extent), 0.01, jnp.float32)
            for m in range(modes):
                place = span(member * modes + m)
                real = spectrum[low, place]
                imag = spectrum[high, place]
                magnitude += real * real + imag * imag
            factor = moduli_ref[q] * lax.rsqrt(magnitude)
            for m in range(modes):
                place = span(member * modes + m)
                scaled.append(
                    stack_up([spectrum[low, place] * factor, spectrum[high, place] * factor]).astype(
                        jnp.bfloat16
                    )
                )
        return side_by_side(scaled)

    def second_half(block, standing):
        returned = dot(backward_ref[...], standing).astype(jnp.bfloat16)
        return stack_up(
            [side_by_side([returned[low, span(w)], returned[high, span(w)]]) for w in range(waves)]
        )

    def leave(block, lying):
        new_wave = dot(lying, forward_ref[...])
        for member, q in members(block):
            row, col = corner(offsets_ref, q)
            here = pl.ds(col, extent)
            sum_real = jnp.zeros((extent, extent), jnp.float32)
            sum_imag = jnp.zeros((extent, extent), jnp.float32)
            for m in range(modes):
                place = span(member * modes + m)
                change_real = new_wave[place, low] - change_ref[q, m, 0]
                change_imag = new_wave[place, high] - change_ref[q, m, 1]
                change_ref[q, m, 0] = change_real
                change_ref[q, m, 1] = change_imag
                probe_real = probe_ref[0, m]
                probe_imag = probe_ref[1, m]
                sum_real += probe_real * change_real + probe_imag * change_imag
                sum_imag += probe_real * change_imag - probe_imag * change_real
            for part, value in enumerate((sum_real, sum_imag)):
                for side, moved in enumerate(spread(value, row)):
                    total[part, side, here] += moved

    stages = [[enter], [first_half], [project], [second_half, leave]]
    blocks = positions // group
    held = [None] * blocks
    for tick in range(blocks + len(stages) - 1):
        for depth in range(len(stages)):
            block = tick - depth
            if not 0 <= block < blocks:
                continue
            for stage in stages[depth]:
                held[block] = stage(block) if stage is enter else stage(block, held[block])

    for part in range(2):
        upper_ref[part] = total[part, 0]
        lower_ref[part] = total[part, 1].astype(jnp.bfloat16)


def share_kernel(change_ref, window_ref, share_ref):
    extent = change_ref.shape[-1]
    positions, modes = change_ref.shape[:2]
    chunk = 32
    for start in range(0, extent, chunk):
        here = pl.ds(start, chunk)
        density = jnp.zeros((chunk, extent), jnp.float32)
        sums = [[jnp.zeros((chunk, extent), jnp.float32) for _ in range(2)] for _ in range(modes)]
        for q in range(positions):
            object_real = window_ref[q, 0, here]
            object_imag = window_ref[q, 1, here]
            density += object_real * object_real + object_imag * object_imag
            for m in range(modes):
                change_real = change_ref[q, m, 0, here]
                change_imag = change_ref[q, m, 1, here]
                sums[m][0] += object_real * change_real + object_imag * change_imag
                sums[m][1] += object_real * change_imag - object_imag * change_real
        for m in range(modes):
            for part in range(2):
                share_ref[part * modes + m, here] = sums[m][part].astype(jnp.bfloat16)
        share_ref[2 * modes, here] = density.astype(jnp.bfloat16)


def weight_kernel(above_ref, power_ref, weight_ref, inverse_ref, other, *, positions):
    extent = power_ref.shape[-1]
    cols = inverse_ref.shape[0]
    power = power_ref[...]
    other[...] = jnp.zeros_like(other)
    line = above_ref[2 * cols :].astype(jnp.float32)
    lane = lax.broadcasted_iota(jnp.int32, line.shape, 1)
    above = [
        jnp.max(jnp.where(lane == k, line, 0.0)).astype(jnp.int32) for k in range(2 * positions)
    ]
    for q in range(positions):
        row = STEP * (q // PCOLS) + above[q]
        col = STEP * (q % PCOLS) + above[positions + q]
        _, right = spread(power, row)
        other[pl.ds(col, extent)] += right
    has_above = lax.axis_index("tile") > 0
    inverse_ref[...] = 1.0 / (weight_ref[...] + jnp.where(has_above, other[...], 0.0))


def object_kernel(object_ref, upper_ref, received_ref, inverse_ref, new_ref, sent_ref):
    has_above = lax.axis_index("tile") > 0
    for part in range(2):
        received = received_ref[part].astype(jnp.float32)
        wave = upper_ref[part] + jnp.where(has_above, received, 0.0)
        value = object_ref[part] + wave * inverse_ref[...]
        new_ref[part] = value
        sent_ref[part] = value.astype(jnp.bfloat16)


def mix_kernel(table_ref, *refs, first, chained, chunk):
    mixed_ref = refs[-1]
    refs = refs[:-1]
    before, own_ref, refs = (refs[0], refs[1], refs[2:]) if chained else (None, None, refs)
    parts, rows, lanes = mixed_ref.shape[1:]
    components, height = table_ref.shape[1:3]
    folded = (chunk // height, height, lanes)
    for part in range(parts):
        for start in range(0, rows, chunk):
            here = pl.ds(start, chunk)
            values = [ref[part, here].astype(jnp.float32).reshape(folded) for ref in refs]
            base = 0.5 * own_ref[part, here].reshape(folded) if chained else None
            for k in range(components):
                terms = [table_ref[first + n, k] * value for n, value in enumerate(values)]
                if chained:
                    terms.insert(0, before[k, part, here].reshape(folded))
                total = functools.reduce(jnp.add, terms)
                mixed_ref[k, part, here] = total.reshape(chunk, lanes)
                if chained:
                    base += total
            if chained:
                mixed_ref[components, part, here] = base.reshape(chunk, lanes)


def finish_kernel(probe_ref, table_ref, last_ref, late_ref, mixed_ref, *refs, first, chunk):
    refs, (out_hbm, probe_hbm, result, sems) = refs[:-4], refs[-4:]
    parts, rows, lanes = mixed_ref.shape[1:]
    components, height = table_ref.shape[1:3]
    folded = (chunk // height, height, lanes)
    copies = [pltpu.make_async_copy(probe_ref, probe_hbm, sems.at[0])]
    copies[0].start()
    for part in range(parts):
        for start in range(0, rows, chunk):
            here = pl.ds(start, chunk)
            values = [ref[part, here].astype(jnp.float32).reshape(folded) for ref in refs]
            found = mixed_ref[components, part, here].reshape(folded)
            for n, value in enumerate(values):
                found += late_ref[first + n] * value
            for k in range(components):
                c = mixed_ref[k, part, here].reshape(folded)
                for n, value in enumerate(values):
                    c += table_ref[first + n, k] * value
                t = last_ref[k]
                found -= jnp.minimum(jnp.maximum(c, -t), t)
            result[part, here] = found.reshape(chunk, lanes)
            source, target = result.at[part, here], out_hbm.at[part, 0, here]
            copies.append(pltpu.make_async_copy(source, target, sems.at[len(copies)]))
            copies[-1].start()
    for copy in copies:
        copy.wait()


def probe_kernel(probe_ref, own_ref, received_ref, new_ref):
    modes = probe_ref.shape[1]
    density = own_ref[2 * modes].astype(jnp.float32) + received_ref[2 * modes].astype(jnp.float32)
    inverse = 1.0 / (density + 0.1 * jnp.max(density) + 1e-06)
    for part in range(2):
        for m in range(modes):
            k = part * modes + m
            numerator = own_ref[k].astype(jnp.float32) + received_ref[k].astype(jnp.float32)
            new_ref[part, m, 0] = (probe_ref[part, m] + numerator * inverse).T


def call(kernel, inputs, places, outputs, scratch=(), limit=4, out="v"):
    kinds = {"s": pltpu.SMEM, "v": pltpu.VMEM, "h": pltpu.HBM}
    inputs = [
        pltpu.with_memory_space_constraint(x, pltpu.HBM) if p == "h" else x
        for x, p in zip(inputs, places)
    ]
    return pl.pallas_call(
        kernel,
        out_shape=outputs,
        in_specs=[pl.BlockSpec(memory_space=kinds[p]) for p in places],
        out_specs=jax.tree.map(lambda _: pl.BlockSpec(memory_space=kinds[out]), outputs),
        scratch_shapes=list(scratch),
        compiler_params=pltpu.CompilerParams(vmem_limit_bytes=limit << 20),
    )(*inputs)


def body(object_field, probe_field, modulus, offsets, spectra_basis, analysis, threshold):
    extent = probe_field.shape[-1]
    modes = probe_field.shape[1]
    object_field = jnp.transpose(object_field, (0, 1, 3, 2))
    offsets = jnp.transpose(offsets)
    cols, rows = object_field.shape[2:]
    positions = offsets.shape[1]
    tiles = lax.axis_size("tile")
    zs = lax.axis_size("energy")
    ms = lax.axis_size("mode")
    forward, backward = dft_tables(extent)
    shape = jax.ShapeDtypeStruct
    f32, bf16 = jnp.float32, jnp.bfloat16

    message, object_here = call(
        round_kernel,
        (offsets, object_field),
        "hh",
        (shape((2 * cols + PAD_ROWS, rows), bf16), shape((2, cols, rows), f32)),
        (pltpu.SMEM((2, positions), jnp.int32), pltpu.SemaphoreType.DMA((3,))),
    )
    if tiles == 2:
        below = above = lax.ppermute(message, "tile", swap_pairs(2, 1))
    else:
        below = lax.ppermute(message, "tile", [(i + 1, i) for i in range(tiles - 1)])
        above = lax.ppermute(message, "tile", [(i, i + 1) for i in range(tiles - 1)])

    near, far = zs - 1, zs // 2
    middle = [dz for dz in range(1, zs) if dz not in (near, far)]
    stages = [
        [(dz, dm) for dz in (0, near) for dm in range(ms)],
        [(dz, dm) for dz in middle for dm in range(ms)] + [(far, 0)],
        [(far, dm) for dm in range(1, ms)],
    ]
    sources = sum(stages, [])
    components = threshold.shape[0]
    offsets, forward, backward, turned, moduli, power, weight, table, last_table, late_table = call(
        functools.partial(turn_kernel, sources=tuple(sources), sizes=(zs, ms)),
        (offsets, analysis, spectra_basis, threshold, forward, backward, probe_field, modulus),
        "hhhhhhhh",
        (
            shape((2, positions), jnp.int32),
            shape(forward.shape, bf16),
            shape(backward.shape, bf16),
            shape((2, modes, extent, extent), f32),
            shape((positions, extent, extent), f32),
            shape((extent, extent), f32),
            shape((cols, rows), f32),
            shape((len(sources), components, 8, LANES), f32),
            shape((components, 8, LANES), f32),
            shape((len(sources), 8, LANES), f32),
        ),
        (
            pltpu.SMEM((2, positions), jnp.int32),
            pltpu.SMEM(analysis.shape, f32),
            pltpu.SMEM(spectra_basis.shape, f32),
            pltpu.SMEM(threshold.shape, f32),
            pltpu.VMEM(probe_field.shape, f32),
            pltpu.VMEM(modulus.shape, bf16),
            pltpu.SemaphoreType.DMA((9,)),
        ),
        limit=8,
    )
    upper, lower, change, window = call(
        functools.partial(wave_kernel, tiles=tiles, group=2),
        (offsets, message, below, turned, moduli, forward, backward),
        "svvvvvv",
        (
            shape((2, cols, rows), f32),
            shape((2, cols, rows), bf16),
            shape((positions, modes, 2, extent, extent), f32),
            shape((positions, 2, extent, extent), f32),
        ),
        (
            pltpu.VMEM((2, 2, cols, LANES), f32),
            pltpu.VMEM((2, 2, cols, LANES), f32),
        ),
        limit=24,
    )
    if tiles == 2:
        received = lax.ppermute(lower, "tile", swap_pairs(2, 1))
    else:
        received = lax.ppermute(lower, "tile", [(i, i + 1) for i in range(tiles - 1)])
    inverse = call(
        functools.partial(weight_kernel, positions=positions),
        (above, power, weight),
        "vvv",
        shape((cols, rows), f32),
        (pltpu.VMEM((cols, rows), f32),),
    )
    share = call(share_kernel, (change, window), "vv", shape((2 * modes + 1, extent, extent), bf16))
    object_new, sent = call(
        object_kernel,
        (object_here, upper, received, inverse),
        "vvvv",
        (shape((2, cols, rows), f32), shape((2, cols, rows), bf16)),
    )
    pieces = {(0, 0): sent}
    for dz in range(1, zs):
        pieces[dz, 0] = lax.ppermute(sent, "energy", swap_pairs(zs, dz))
    for dz in range(zs):
        for dm in range(1, ms):
            pieces[dz, dm] = lax.ppermute(pieces[dz, 0], "mode", swap_pairs(ms, dm))
    mixed = None
    first = 0
    for number, stage in enumerate(stages[:2]):
        before = [] if mixed is None else [mixed, object_new]
        inputs = [table] + before + [pieces[s] for s in stage]
        mixed = call(
            functools.partial(mix_kernel, first=first, chained=mixed is not None, chunk=64),
            inputs,
            "v" * len(inputs),
            shape((components + number, 2, cols, rows), f32),
        )
        first += len(stage)
    for distance in [1 << k for k in range(1, tiles.bit_length() - 1)]:
        other = lax.ppermute(share, "tile", swap_pairs(tiles, distance))
        share = (share.astype(f32) + other.astype(f32)).astype(bf16)
    other = lax.ppermute(share, "tile", swap_pairs(tiles, 1))
    probe_new = call(probe_kernel, (turned, share, other), "vvv", shape(probe_field.shape, f32))
    inputs = [probe_new, table, last_table, late_table, mixed] + [pieces[s] for s in stages[2]]
    object_out, probe_out = call(
        functools.partial(finish_kernel, first=first, chunk=64),
        inputs,
        "v" * len(inputs),
        (shape(object_field.shape, f32), shape(probe_field.shape, f32)),
        (pltpu.VMEM((2, cols, rows), f32), pltpu.SemaphoreType.DMA((1 + 2 * cols // 64,))),
        out="h",
    )
    return (jnp.transpose(object_out, (0, 1, 3, 2)), probe_out)


def solution(mesh):
    placed = (
        P(None, ("groups", "energy", "mode"), "tile", None),
        P(None, None, ("groups", "energy", "mode"), None, None),
        P(("groups", "energy", "mode"), "tile", None, None),
        P(("groups", "tile"), None),
        P(),
        P(),
        P(),
    )
    return jax.shard_map(
        body,
        mesh=mesh,
        in_specs=placed,
        out_specs=(
            P(None, ("groups", "energy", "mode"), "tile", None),
            P(None, None, ("groups", "energy", "mode"), None, None),
        ),
        check_vma=False,
    )
```

```python
import functools
import math

import jax
import jax.numpy as jnp
import ml_dtypes
import numpy as np
from jax import lax
from jax.experimental import pallas as pl
from jax.experimental.pallas import tpu as pltpu
from jax.sharding import PartitionSpec as P

PCOLS = 2
STEP = 32
LANES = 128
PAD_ROWS = 8


def swap_pairs(size, distance):
    return [(i, i ^ distance) for i in range(size)]


def dft_tables(extent):
    counter = np.arange(extent)
    phases = -2.0 * math.pi / extent * (counter[:, None] * counter[None, :] % extent)
    cosine = np.cos(phases) / math.sqrt(extent)
    sine = np.sin(phases) / math.sqrt(extent)
    forward = np.block([[cosine, -sine], [sine, cosine]])
    backward = np.block([[cosine, sine], [-sine, cosine]])
    return (
        jnp.asarray(forward.astype(np.float32).astype(ml_dtypes.bfloat16)),
        jnp.asarray(backward.astype(np.float32).astype(ml_dtypes.bfloat16)),
    )


def corner(offsets, q):
    row = STEP * (q // PCOLS) + offsets[0, q]
    col = STEP * (q % PCOLS) + offsets[1, q]
    return row, col


def spread(block, row):
    lane = lax.broadcasted_iota(jnp.int32, block.shape, 1)
    turned = pltpu.roll(block, row, 1)
    left = jnp.where(lane >= row, turned, 0.0)
    right = jnp.where(lane < row, turned, 0.0)
    return left, right


def round_kernel(offsets_hbm, object_hbm, message_ref, object_ref, offsets_ref, sems):
    cols, rows = object_ref.shape[1:]
    positions = offsets_ref.shape[1]
    copies = [pltpu.make_async_copy(offsets_hbm, offsets_ref, sems.at[2])]
    copies += [
        pltpu.make_async_copy(object_hbm.at[part, 0], object_ref.at[part], sems.at[part])
        for part in range(2)
    ]
    for copy in copies:
        copy.start()
    for part in range(2):
        copies[1 + part].wait()
        message_ref[part * cols : (part + 1) * cols] = object_ref[part].astype(jnp.bfloat16)
    copies[0].wait()
    lane = lax.broadcasted_iota(jnp.int32, (PAD_ROWS, rows), 1)
    line = jnp.zeros((PAD_ROWS, rows), jnp.float32)
    for k in range(2):
        for q in range(positions):
            value = offsets_ref[k, q].astype(jnp.float32)
            line = jnp.where(lane == k * positions + q, value, line)
    message_ref[2 * cols :] = line.astype(jnp.bfloat16)


def turn_kernel(
    offsets_hbm,
    analysis_hbm,
    basis_hbm,
    threshold_hbm,
    forward_hbm,
    backward_hbm,
    probe_hbm,
    moduli_hbm,
    offsets_out_ref,
    forward_ref,
    backward_ref,
    turned_ref,
    moduli_out_ref,
    power_ref,
    weight_ref,
    analysis_table_ref,
    last_table_ref,
    late_table_ref,
    offsets_ref,
    analysis_ref,
    basis_ref,
    threshold_ref,
    probe_ref,
    moduli_ref,
    sems,
    *,
    sources,
    sizes,
):
    modes = probe_ref.shape[1]
    extent = probe_ref.shape[-1]
    positions = offsets_ref.shape[1]
    pairs = [
        (offsets_hbm, offsets_ref),
        (probe_hbm, probe_ref),
        (moduli_hbm, moduli_ref),
        (analysis_hbm, analysis_ref),
        (basis_hbm, basis_ref),
        (threshold_hbm, threshold_ref),
        (forward_hbm, forward_ref),
        (backward_hbm, backward_ref),
        (offsets_hbm, offsets_out_ref),
    ]
    copies = [
        pltpu.make_async_copy(source, target, sems.at[k])
        for k, (source, target) in enumerate(pairs)
    ]
    for copy in copies:
        copy.start()
    for copy in copies[3:6]:
        copy.wait()
    _, ms = sizes
    z = lax.axis_index("energy")
    m = lax.axis_index("mode")
    tile = analysis_table_ref.shape[2:]
    late = [0.0] * len(sources)
    for k in range(threshold_ref.shape[0]):
        half = 0.5 * basis_ref[z * ms + m, k]
        for number, (dz, dm) in enumerate(sources):
            label = (z ^ dz) * ms + (m ^ dm)
            weight = half * analysis_ref[k, label]
            analysis_table_ref[number, k] = jnp.full(tile, weight)
            late[number] += weight
        last_table_ref[k] = jnp.full(tile, jnp.maximum(half, -half) * threshold_ref[k])
    for number in range(len(sources)):
        late_table_ref[number] = jnp.full(tile, late[number])
    copies[0].wait()
    copies[1].wait()
    power = jnp.zeros((extent, extent), jnp.float32)
    for part in range(2):
        for m in range(modes):
            value = probe_ref[part, m, 0].T
            turned_ref[part, m] = value
            power += value * value
    power_ref[...] = power
    weight_ref[...] = jnp.full_like(weight_ref, 0.1 * jnp.max(power) + 1e-06)
    for q in range(positions):
        row, col = corner(offsets_ref, q)
        left, _ = spread(power, row)
        weight_ref[pl.ds(col, extent)] += left
    copies[2].wait()
    for q in range(positions):
        moduli_out_ref[q] = moduli_ref[0, q].astype(jnp.float32).T
    for copy in copies[6:]:
        copy.wait()


def cut(extended, offsets_ref, q, extent):
    row, col = corner(offsets_ref, q)
    here = pl.ds(col, extent)
    lane = lax.broadcasted_iota(jnp.int32, (extent, extent), 1)
    found = []
    amount = lax.rem(extent - row, extent)
    for part in range(2):
        left = pltpu.roll(extended[part, 0, here], amount, 1)
        right = pltpu.roll(extended[part, 1, here], amount, 1)
        found.append(jnp.where(lane < extent - row, left, right))
    return found


def extend(extended, own_ref, below_ref, tiles):
    cols = extended.shape[2]
    has_below = lax.axis_index("tile") < tiles - 1
    for part in range(2):
        here = slice(part * cols, (part + 1) * cols)
        extended[part, 0] = own_ref[here].astype(jnp.float32)
        extended[part, 1] = jnp.where(has_below, below_ref[here].astype(jnp.float32), 0.0)


def side_by_side(blocks):
    return jnp.concatenate(blocks, axis=1)


def stack_up(blocks):
    return jnp.concatenate(blocks, axis=0)


def wave_kernel(
    offsets_ref,
    own_ref,
    below_ref,
    probe_ref,
    moduli_ref,
    forward_ref,
    backward_ref,
    sums_ref,
    lower_ref,
    change_ref,
    window_ref,
    extended,
    total,
    *,
    tiles,
    group,
):
    extent = probe_ref.shape[-1]
    modes = probe_ref.shape[1]
    positions = offsets_ref.shape[1]
    waves = group * modes
    extend(extended, own_ref, below_ref, tiles)
    total[...] = jnp.zeros_like(total)
    low = slice(0, extent)
    high = slice(extent, 2 * extent)

    def dot(left, right):
        return jnp.dot(left, right, preferred_element_type=jnp.float32)

    def span(w):
        return slice(w * extent, (w + 1) * extent)

    def members(block):
        return [(member, block * group + member) for member in range(group)]

    def enter(block):
        rounded = []
        for member, q in members(block):
            object_real, object_imag = cut(extended, offsets_ref, q, extent)
            window_ref[q, 0] = object_real
            window_ref[q, 1] = object_imag
            for m in range(modes):
                probe_real = probe_ref[0, m]
                probe_imag = probe_ref[1, m]
                wave_real = probe_real * object_real - probe_imag * object_imag
                wave_imag = probe_real * object_imag + probe_imag * object_real
                change_ref[q, m, 0] = wave_real
                change_ref[q, m, 1] = wave_imag
                rounded.append(side_by_side([wave_real, wave_imag]).astype(jnp.bfloat16))
        return stack_up(rounded)

    def first_half(block, lying):
        halfway = dot(lying, backward_ref[...]).astype(jnp.bfloat16)
        return side_by_side(
            [stack_up([halfway[span(w), low], halfway[span(w), high]]) for w in range(waves)]
        )

    def project(block, standing):
        spectrum = dot(forward_ref[...], standing)
        scaled = []
        for member, q in members(block):
            magnitude = jnp.full((extent, extent), 0.01, jnp.float32)
            for m in range(modes):
                place = span(member * modes + m)
                real = spectrum[low, place]
                imag = spectrum[high, place]
                magnitude += real * real + imag * imag
            factor = moduli_ref[q] * lax.rsqrt(magnitude)
            for m in range(modes):
                place = span(member * modes + m)
                scaled.append(
                    stack_up([spectrum[low, place] * factor, spectrum[high, place] * factor]).astype(
                        jnp.bfloat16
                    )
                )
        return side_by_side(scaled)

    def second_half(block, standing):
        returned = dot(backward_ref[...], standing).astype(jnp.bfloat16)
        return stack_up(
            [side_by_side([returned[low, span(w)], returned[high, span(w)]]) for w in range(waves)]
        )

    def leave(block, lying):
        new_wave = dot(lying, forward_ref[...])
        for member, q in members(block):
            row, col = corner(offsets_ref, q)
            here = pl.ds(col, extent)
            sum_real = jnp.zeros((extent, extent), jnp.float32)
            sum_imag = jnp.zeros((extent, extent), jnp.float32)
            for m in range(modes):
                place = span(member * modes + m)
                change_real = new_wave[place, low] - change_ref[q, m, 0]
                change_imag = new_wave[place, high] - change_ref[q, m, 1]
                change_ref[q, m, 0] = change_real
                change_ref[q, m, 1] = change_imag
                probe_real = probe_ref[0, m]
                probe_imag = probe_ref[1, m]
                sum_real += probe_real * change_real + probe_imag * change_imag
                sum_imag += probe_real * change_imag - probe_imag * change_real
            for part, value in enumerate((sum_real, sum_imag)):
                sums_ref[q, part] = value
                _, right = spread(value, row)
                total[part, here] += right

    stages = [[enter], [first_half], [project], [second_half, leave]]
    blocks = positions // group
    held = [None] * blocks
    for tick in range(blocks + len(stages) - 1):
        for depth in (1, 0, 2, 3):
            block = tick - depth
            if not 0 <= block < blocks:
                continue
            for stage in stages[depth]:
                held[block] = stage(block) if stage is enter else stage(block, held[block])

    for part in range(2):
        lower_ref[part] = total[part].astype(jnp.bfloat16)


def upper_kernel(offsets_ref, sums_ref, upper_ref):
    extent = sums_ref.shape[-1]
    upper_ref[...] = jnp.zeros_like(upper_ref)
    for q in range(sums_ref.shape[0]):
        row, col = corner(offsets_ref, q)
        here = pl.ds(col, extent)
        for part in range(2):
            left, _ = spread(sums_ref[q, part], row)
            upper_ref[part, here] += left


def share_kernel(change_ref, window_ref, share_ref):
    extent = change_ref.shape[-1]
    positions, modes = change_ref.shape[:2]
    chunk = 32
    for start in range(0, extent, chunk):
        here = pl.ds(start, chunk)
        density = jnp.zeros((chunk, extent), jnp.float32)
        sums = [[jnp.zeros((chunk, extent), jnp.float32) for _ in range(2)] for _ in range(modes)]
        for q in range(positions):
            object_real = window_ref[q, 0, here]
            object_imag = window_ref[q, 1, here]
            density += object_real * object_real + object_imag * object_imag
            for m in range(modes):
                change_real = change_ref[q, m, 0, here]
                change_imag = change_ref[q, m, 1, here]
                sums[m][0] += object_real * change_real + object_imag * change_imag
                sums[m][1] += object_real * change_imag - object_imag * change_real
        for m in range(modes):
            for part in range(2):
                share_ref[part * modes + m, here] = sums[m][part].astype(jnp.bfloat16)
        share_ref[2 * modes, here] = density.astype(jnp.bfloat16)


def weight_kernel(above_ref, power_ref, weight_ref, inverse_ref, other, *, positions):
    extent = power_ref.shape[-1]
    cols = inverse_ref.shape[0]
    power = power_ref[...]
    other[...] = jnp.zeros_like(other)
    line = above_ref[2 * cols :].astype(jnp.float32)
    lane = lax.broadcasted_iota(jnp.int32, line.shape, 1)
    above = [
        jnp.max(jnp.where(lane == k, line, 0.0)).astype(jnp.int32) for k in range(2 * positions)
    ]
    for q in range(positions):
        row = STEP * (q // PCOLS) + above[q]
        col = STEP * (q % PCOLS) + above[positions + q]
        _, right = spread(power, row)
        other[pl.ds(col, extent)] += right
    has_above = lax.axis_index("tile") > 0
    inverse_ref[...] = 1.0 / (weight_ref[...] + jnp.where(has_above, other[...], 0.0))


def object_kernel(object_ref, upper_ref, received_ref, inverse_ref, new_ref, sent_ref):
    has_above = lax.axis_index("tile") > 0
    for part in range(2):
        received = received_ref[part].astype(jnp.float32)
        wave = upper_ref[part] + jnp.where(has_above, received, 0.0)
        value = object_ref[part] + wave * inverse_ref[...]
        new_ref[part] = value
        sent_ref[part] = value.astype(jnp.bfloat16)


def mix_kernel(table_ref, *refs, first, chained, chunk):
    mixed_ref = refs[-1]
    refs = refs[:-1]
    before, own_ref, refs = (refs[0], refs[1], refs[2:]) if chained else (None, None, refs)
    parts, rows, lanes = mixed_ref.shape[1:]
    components, height = table_ref.shape[1:3]
    folded = (chunk // height, height, lanes)
    for part in range(parts):
        for start in range(0, rows, chunk):
            here = pl.ds(start, chunk)
            values = [ref[part, here].astype(jnp.float32).reshape(folded) for ref in refs]
            base = 0.5 * own_ref[part, here].reshape(folded) if chained else None
            for k in range(components):
                terms = [table_ref[first + n, k] * value for n, value in enumerate(values)]
                if chained:
                    terms.insert(0, before[k, part, here].reshape(folded))
                total = functools.reduce(jnp.add, terms)
                mixed_ref[k, part, here] = total.reshape(chunk, lanes)
                if chained:
                    base += total
            if chained:
                mixed_ref[components, part, here] = base.reshape(chunk, lanes)


def finish_kernel(probe_ref, table_ref, last_ref, late_ref, mixed_ref, *refs, first, chunk):
    refs, (out_hbm, probe_hbm, result, sems) = refs[:-4], refs[-4:]
    parts, rows, lanes = mixed_ref.shape[1:]
    components, height = table_ref.shape[1:3]
    folded = (chunk // height, height, lanes)
    copies = [pltpu.make_async_copy(probe_ref, probe_hbm, sems.at[0])]
    copies[0].start()
    for part in range(parts):
        for start in range(0, rows, chunk):
            here = pl.ds(start, chunk)
            values = [ref[part, here].astype(jnp.float32).reshape(folded) for ref in refs]
            found = mixed_ref[components, part, here].reshape(folded)
            for n, value in enumerate(values):
                found += late_ref[first + n] * value
            for k in range(components):
                c = mixed_ref[k, part, here].reshape(folded)
                for n, value in enumerate(values):
                    c += table_ref[first + n, k] * value
                t = last_ref[k]
                found -= jnp.minimum(jnp.maximum(c, -t), t)
            result[part, here] = found.reshape(chunk, lanes)
            source, target = result.at[part, here], out_hbm.at[part, 0, here]
            copies.append(pltpu.make_async_copy(source, target, sems.at[len(copies)]))
            copies[-1].start()
    for copy in copies:
        copy.wait()


def probe_kernel(probe_ref, own_ref, received_ref, new_ref):
    modes = probe_ref.shape[1]
    density = own_ref[2 * modes].astype(jnp.float32) + received_ref[2 * modes].astype(jnp.float32)
    inverse = 1.0 / (density + 0.1 * jnp.max(density) + 1e-06)
    for part in range(2):
        for m in range(modes):
            k = part * modes + m
            numerator = own_ref[k].astype(jnp.float32) + received_ref[k].astype(jnp.float32)
            new_ref[part, m, 0] = (probe_ref[part, m] + numerator * inverse).T


def call(kernel, inputs, places, outputs, scratch=(), limit=4, out="v"):
    kinds = {"s": pltpu.SMEM, "v": pltpu.VMEM, "h": pltpu.HBM}
    inputs = [
        pltpu.with_memory_space_constraint(x, pltpu.HBM) if p == "h" else x
        for x, p in zip(inputs, places)
    ]
    return pl.pallas_call(
        kernel,
        out_shape=outputs,
        in_specs=[pl.BlockSpec(memory_space=kinds[p]) for p in places],
        out_specs=jax.tree.map(lambda _: pl.BlockSpec(memory_space=kinds[out]), outputs),
        scratch_shapes=list(scratch),
        compiler_params=pltpu.CompilerParams(vmem_limit_bytes=limit << 20),
    )(*inputs)


def body(object_field, probe_field, modulus, offsets, spectra_basis, analysis, threshold):
    extent = probe_field.shape[-1]
    modes = probe_field.shape[1]
    object_field = jnp.transpose(object_field, (0, 1, 3, 2))
    offsets = jnp.transpose(offsets)
    cols, rows = object_field.shape[2:]
    positions = offsets.shape[1]
    tiles = lax.axis_size("tile")
    zs = lax.axis_size("energy")
    ms = lax.axis_size("mode")
    forward, backward = dft_tables(extent)
    shape = jax.ShapeDtypeStruct
    f32, bf16 = jnp.float32, jnp.bfloat16

    message, object_here = call(
        round_kernel,
        (offsets, object_field),
        "hh",
        (shape((2 * cols + PAD_ROWS, rows), bf16), shape((2, cols, rows), f32)),
        (pltpu.SMEM((2, positions), jnp.int32), pltpu.SemaphoreType.DMA((3,))),
    )
    if tiles == 2:
        below = above = lax.ppermute(message, "tile", swap_pairs(2, 1))
    else:
        below = lax.ppermute(message, "tile", [(i + 1, i) for i in range(tiles - 1)])
        above = lax.ppermute(message, "tile", [(i, i + 1) for i in range(tiles - 1)])

    near, far = zs - 1, zs // 2
    middle = [dz for dz in range(1, zs) if dz not in (near, far)]
    stages = [
        [(dz, dm) for dz in (0, near) for dm in range(ms)],
        [(dz, dm) for dz in middle for dm in range(ms)] + [(far, 0)],
        [(far, dm) for dm in range(1, ms)],
    ]
    sources = sum(stages, [])
    components = threshold.shape[0]
    offsets, forward, backward, turned, moduli, power, weight, table, last_table, late_table = call(
        functools.partial(turn_kernel, sources=tuple(sources), sizes=(zs, ms)),
        (offsets, analysis, spectra_basis, threshold, forward, backward, probe_field, modulus),
        "hhhhhhhh",
        (
            shape((2, positions), jnp.int32),
            shape(forward.shape, bf16),
            shape(backward.shape, bf16),
            shape((2, modes, extent, extent), f32),
            shape((positions, extent, extent), f32),
            shape((extent, extent), f32),
            shape((cols, rows), f32),
            shape((len(sources), components, 8, LANES), f32),
            shape((components, 8, LANES), f32),
            shape((len(sources), 8, LANES), f32),
        ),
        (
            pltpu.SMEM((2, positions), jnp.int32),
            pltpu.SMEM(analysis.shape, f32),
            pltpu.SMEM(spectra_basis.shape, f32),
            pltpu.SMEM(threshold.shape, f32),
            pltpu.VMEM(probe_field.shape, f32),
            pltpu.VMEM(modulus.shape, bf16),
            pltpu.SemaphoreType.DMA((9,)),
        ),
        limit=8,
    )
    sums, lower, change, window = call(
        functools.partial(wave_kernel, tiles=tiles, group=2),
        (offsets, message, below, turned, moduli, forward, backward),
        "svvvvvv",
        (
            shape((positions, 2, extent, extent), f32),
            shape((2, cols, rows), bf16),
            shape((positions, modes, 2, extent, extent), f32),
            shape((positions, 2, extent, extent), f32),
        ),
        (
            pltpu.VMEM((2, 2, cols, LANES), f32),
            pltpu.VMEM((2, cols, rows), f32),
        ),
        limit=24,
    )
    if tiles == 2:
        received = lax.ppermute(lower, "tile", swap_pairs(2, 1))
    else:
        received = lax.ppermute(lower, "tile", [(i, i + 1) for i in range(tiles - 1)])
    inverse = call(
        functools.partial(weight_kernel, positions=positions),
        (above, power, weight),
        "vvv",
        shape((cols, rows), f32),
        (pltpu.VMEM((cols, rows), f32),),
    )
    share = call(share_kernel, (change, window), "vv", shape((2 * modes + 1, extent, extent), bf16))
    upper = call(upper_kernel, (offsets, sums), "sv", shape((2, cols, rows), f32))
    object_new, sent = call(
        object_kernel,
        (object_here, upper, received, inverse),
        "vvvv",
        (shape((2, cols, rows), f32), shape((2, cols, rows), bf16)),
    )
    pieces = {(0, 0): sent}
    for dz in range(1, zs):
        pieces[dz, 0] = lax.ppermute(sent, "energy", swap_pairs(zs, dz))
    for dz in range(zs):
        for dm in range(1, ms):
            pieces[dz, dm] = lax.ppermute(pieces[dz, 0], "mode", swap_pairs(ms, dm))
    mixed = None
    first = 0
    for number, stage in enumerate(stages[:2]):
        before = [] if mixed is None else [mixed, object_new]
        inputs = [table] + before + [pieces[s] for s in stage]
        mixed = call(
            functools.partial(mix_kernel, first=first, chained=mixed is not None, chunk=64),
            inputs,
            "v" * len(inputs),
            shape((components + number, 2, cols, rows), f32),
        )
        first += len(stage)
    for distance in [1 << k for k in range(1, tiles.bit_length() - 1)]:
        other = lax.ppermute(share, "tile", swap_pairs(tiles, distance))
        share = (share.astype(f32) + other.astype(f32)).astype(bf16)
    other = lax.ppermute(share, "tile", swap_pairs(tiles, 1))
    probe_new = call(probe_kernel, (turned, share, other), "vvv", shape(probe_field.shape, f32))
    inputs = [probe_new, table, last_table, late_table, mixed] + [pieces[s] for s in stages[2]]
    object_out, probe_out = call(
        functools.partial(finish_kernel, first=first, chunk=64),
        inputs,
        "v" * len(inputs),
        (shape(object_field.shape, f32), shape(probe_field.shape, f32)),
        (pltpu.VMEM((2, cols, rows), f32), pltpu.SemaphoreType.DMA((1 + 2 * cols // 64,))),
        out="h",
    )
    return (jnp.transpose(object_out, (0, 1, 3, 2)), probe_out)


def solution(mesh):
    placed = (
        P(None, ("groups", "energy", "mode"), "tile", None),
        P(None, None, ("groups", "energy", "mode"), None, None),
        P(("groups", "energy", "mode"), "tile", None, None),
        P(("groups", "tile"), None),
        P(),
        P(),
        P(),
    )
    return jax.shard_map(
        body,
        mesh=mesh,
        in_specs=placed,
        out_specs=(
            P(None, ("groups", "energy", "mode"), "tile", None),
            P(None, None, ("groups", "energy", "mode"), None, None),
        ),
        check_vma=False,
    )
```
